256 devices in a mesh: segment: 2 (over z_lo), tm: 16 (over x, z_hi), space: 8 (over y, core).
Axes of the slice: x: 4, y: 4, z: 8 (z_hi: 4, z_lo: 2; z = z_hi * 2 + z_lo), core: 2. Of those that a mesh axis runs over, the one named last changes fastest.
Arguments:
- clip_frames: bfloat16 [64, 64, 128, 128], P('tm', 'space'), may hold values from -6 to 6
- enc_weight: bfloat16 [3, 3, 3, 128, 256], replicated, may hold values from -0.109375 to 0.109375
- dec_weight: bfloat16 [3, 3, 3, 256, 128], replicated, may hold values from -0.078125 to 0.078125
- out_grad: bfloat16 [32, 32, 64, 128], P('tm', 'space'), may hold values from -6 to 6
Outputs:
- latent_pair: bfloat16 [2, 32, 32, 64, 256], P('segment', 'tm', 'space')
- weight_grads: float32 [2, 27, 32768], P('segment')
The draws below stay inside these ranges and needn't reach their ends.
All inputs are finite; a program needn't handle non-finite values.
Results may differ from the reference program's by a relative error of at most 0.0056.
Values may be sent and summed in bfloat16 or wider, within the bound.
No kernel may reach another device: no remote copies, remote signals or barrier semaphores. Data moves between devices by JAX's collectives and lax.ppermute only.
A program may use at most 128 MiB of HBM per device.

```python
import math
import jax
import jax.numpy as jnp
from jax import lax

C_IN = 128
C_LAT = 256
WL = 64
TL = 32
HL = 32
T_IN = 64
H_IN = 64
W_IN = 128


def block_scale(own_key, dims, cuts, smallest, largest):
    def one(position, shards_of):
        draws = jax.random.uniform(jax.random.fold_in(jax.random.fold_in(own_key, 6), position), (shards_of,), jnp.float32, smallest / len(cuts), largest / len(cuts))
        return jnp.repeat(jnp.exp(draws), dims[position] // shards_of).reshape((-1,) + (1,) * (len(dims) - position - 1))

    factor_of = one(*cuts[0])
    for cut in cuts[1:]:
        factor_of = factor_of * one(*cut)
    return factor_of


def bell_draw(own_key, shape, spread, bound, cuts=(), held_as=jnp.bfloat16):
    entries = jax.random.normal(own_key, shape, jnp.float32) * spread
    if len(cuts) > 0:
        entries = block_scale(own_key, shape, cuts, -0.22, 0.18) * entries
    return jnp.clip(entries, min=-bound, max=bound).astype(held_as)


def setup_inputs(seed: int = 0) -> dict:
    arg_keys = jax.random.split(jax.random.key(seed), 5)
    return {
        "clip_frames": bell_draw(arg_keys[0], (T_IN, H_IN, W_IN, C_IN), 1.0, 6.0, ((0, 16), (1, 8))),
        "enc_weight": bell_draw(arg_keys[1], (3, 3, 3, C_IN, C_LAT), (27 * C_IN) ** -0.5, 0.109375),
        "dec_weight": bell_draw(arg_keys[2], (3, 3, 3, C_LAT, C_IN), (27 * C_LAT) ** -0.5, 0.078125),
        "out_grad": bell_draw(arg_keys[3], (TL, HL, WL, C_IN), 1.0, 6.0, ((0, 16), (1, 8))),
    }


def encode_taps(padded, enc_weight, frame_count, row_count, col_count):
    chans = padded.shape[-1]
    summed = jnp.zeros((frame_count * row_count * col_count, enc_weight.shape[-1]), jnp.float32)
    for tap_t in range(3):
        for tap_h in range(3):
            for tap_w in range(3):
                window = padded[tap_t:tap_t + 2 * frame_count:2, tap_h:tap_h + 2 * row_count:2, tap_w:tap_w + 2 * col_count:2]
                summed = summed + jnp.dot(window.reshape(-1, chans), enc_weight[tap_t, tap_h, tap_w], preferred_element_type=jnp.float32)
    return summed.reshape(frame_count, row_count, col_count, -1).astype(jnp.bfloat16)

def decode_taps(extended, dec_weight, out_grad):
    frame_count, row_count, col_count, out_chans = out_grad.shape
    chans = extended.shape[-1]
    pre_act = jnp.zeros((frame_count * row_count * col_count, out_chans), jnp.float32)
    for tap_t in range(3):
        for tap_h in range(3):
            for tap_w in range(3):
                window = extended[tap_t:tap_t + frame_count, tap_h:tap_h + row_count, tap_w:tap_w + col_count]
                pre_act = pre_act + jnp.dot(window.reshape(-1, chans), dec_weight[tap_t, tap_h, tap_w], preferred_element_type=jnp.float32)
    sigm = jax.nn.sigmoid(pre_act)
    slope = out_grad.reshape(-1, out_chans).astype(jnp.float32) * sigm * (1.0 + pre_act * (1.0 - sigm))
    return slope.astype(jnp.bfloat16).reshape(out_grad.shape)

def transpose_taps(rimmed, dec_weight, frame_count, row_count, col_count):
    chans = rimmed.shape[-1]
    summed = jnp.zeros((frame_count * row_count * col_count, dec_weight.shape[3]), jnp.float32)
    for tap_t in range(3):
        for tap_h in range(3):
            for tap_w in range(3):
                window = rimmed[2 - tap_t:2 - tap_t + frame_count, 2 - tap_h:2 - tap_h + row_count, 2 - tap_w:2 - tap_w + col_count]
                summed = summed + lax.dot_general(window.reshape(-1, chans), dec_weight[tap_t, tap_h, tap_w], (((1,), (1,)), ((), ())), preferred_element_type=jnp.float32)
    return summed.reshape(frame_count, row_count, col_count, -1).astype(jnp.bfloat16)

def enc_taps_grad(padded, lat_grad):
    frame_count, row_count, col_count, lat_chans = lat_grad.shape
    chans = padded.shape[-1]
    flat_grad = lat_grad.reshape(-1, lat_chans)
    pieces = []
    for tap_t in range(3):
        for tap_h in range(3):
            for tap_w in range(3):
                window = padded[tap_t:tap_t + 2 * frame_count:2, tap_h:tap_h + 2 * row_count:2, tap_w:tap_w + 2 * col_count:2]
                pieces.append(lax.dot_general(window.reshape(-1, chans), flat_grad, (((0,), (0,)), ((), ())), preferred_element_type=jnp.float32).reshape(-1))
    return jnp.stack(pieces)

def dec_taps_grad(extended, slope):
    frame_count, row_count, col_count, out_chans = slope.shape
    chans = extended.shape[-1]
    flat_slope = slope.reshape(-1, out_chans)
    pieces = []
    for tap_t in range(3):
        for tap_h in range(3):
            for tap_w in range(3):
                window = extended[tap_t:tap_t + frame_count, tap_h:tap_h + row_count, tap_w:tap_w + col_count]
                pieces.append(lax.dot_general(window.reshape(-1, chans), flat_slope, (((0,), (0,)), ((), ())), preferred_element_type=jnp.float32).reshape(-1))
    return jnp.stack(pieces)

def reference(clip_frames, enc_weight, dec_weight, out_grad):
    padded = jnp.pad(clip_frames, ((2, 0), (1, 1), (1, 1), (0, 0)))
    latent = encode_taps(padded, enc_weight, TL, HL, WL)
    extended = jnp.pad(latent, ((2, 0), (1, 1), (1, 1), (0, 0)))
    slope = decode_taps(extended, dec_weight, out_grad)
    rimmed = jnp.pad(slope, ((0, 2), (1, 1), (1, 1), (0, 0)))
    lat_grad = transpose_taps(rimmed, dec_weight, TL, HL, WL)
    enc_grad = enc_taps_grad(padded, lat_grad)
    dec_grad = dec_taps_grad(extended, slope)
    grad_scale = 1.0 / math.sqrt(TL * HL * WL)
    weight_grads = jnp.stack([enc_grad, dec_grad]) * grad_scale
    latent_pair = jnp.stack([lat_grad, latent])
    return (latent_pair, weight_grads)
```

```python
import math

import jax
import jax.numpy as jnp
from jax import lax
from jax.experimental import pallas as pl
from jax.experimental.pallas import tpu as pltpu
from jax.sharding import PartitionSpec as P

F32 = jnp.float32
BF16 = jnp.bfloat16
PART = BF16
VMEM_LIMIT = 56 * 1024 * 1024


def shape(dims, dtype):
    return jax.ShapeDtypeStruct(dims, dtype)


def on_chip(body, outs, name, smem=0, scratch=()):
    def call(*args):
        specs = [pl.BlockSpec(memory_space=pltpu.SMEM)] * smem
        specs += [pl.BlockSpec(memory_space=pltpu.VMEM)] * (len(args) - smem)
        return pl.pallas_call(
            body,
            out_shape=outs,
            in_specs=specs,
            out_specs=[pl.BlockSpec(memory_space=pltpu.VMEM)] * len(outs),
            scratch_shapes=list(scratch),
            name=name,
            compiler_params=pltpu.CompilerParams(vmem_limit_bytes=VMEM_LIMIT),
        )(*args)

    return call


def dot(left, right):
    return jnp.dot(left, right, preferred_element_type=F32)


def dot_tn(left, right):
    return lax.dot_general(left, right, (((0,), (0,)), ((), ())), preferred_element_type=F32)


def dot_nt(left, right):
    return lax.dot_general(left, right, (((1,), (1,)), ((), ())), preferred_element_type=F32)


def clip_windows(row, stage):
    stage[8:136, :] = row.astype(F32)
    before = stage[pl.ds(7, 64, stride=2), :]
    here = stage[pl.ds(8, 64, stride=2), :]
    after = stage[pl.ds(9, 64, stride=2), :]
    return jnp.concatenate([before, here, after], axis=1).astype(BF16)


def neighbour_cols(row):
    wide = row.astype(F32)
    place = lax.broadcasted_iota(jnp.int32, wide.shape, 0)
    last = wide.shape[0] - 1
    before = jnp.where(place == 0, 0.0, pltpu.roll(wide, 1, 0)).astype(BF16)
    after = jnp.where(place == last, 0.0, pltpu.roll(wide, last, 0)).astype(BF16)
    return before, row, after


def fill_clip(stage, src, top, dst, frames):
    stage[0:8, :] = jnp.zeros((8, stage.shape[1]), F32)
    for f in range(frames):
        dst[f, 0] = clip_windows(top[f, 0], stage)

        def one(r, carry, f=f):
            dst[f, r + 1] = clip_windows(src[f, r], stage)
            return carry

        lax.fori_loop(0, 8, one, 0)


def clip_im2col(taps, f, b):
    return jnp.concatenate([taps[f, 2 * h + b] for h in range(4)], axis=0)


def encode_body(clip, top, weight, lat1, part, own0, taps, stage):
    fill_clip(stage, clip, top, taps, 4)

    def conv(f, a):
        total = None
        for b in range(3):
            term = dot(clip_im2col(taps, f, b), weight[a, b].reshape(384, 256))
            total = term if total is None else total + term
        return total

    lat1[...] = (conv(0, 0) + conv(1, 1) + conv(2, 2)).astype(BF16).reshape(4, 64, 256)
    part[...] = (conv(2, 0) + conv(3, 1)).astype(part.dtype).reshape(4, 64, 256)
    own0[...] = conv(0, 2).reshape(4, 64, 256)


def decode_body(
    p0, p1, o0, o1, pt0, pt1, t0, t1, pb0, pb1, b0, b1, weight, cot, slope, wide
):
    frames = ((p0, pt0, pb0), (p1, pt1, pb1), (o0, t0, b0), (o1, t1, b1))
    for f, (mid, top, bottom) in enumerate(frames):
        wide[f, 0] = jnp.concatenate(neighbour_cols(top[0]), axis=1)
        wide[f, 5] = jnp.concatenate(neighbour_cols(bottom[0]), axis=1)

        def one(r, carry, f=f, mid=mid):
            wide[f, r + 1] = jnp.concatenate(neighbour_cols(mid[r]), axis=1)
            return carry

        lax.fori_loop(0, 4, one, 0)
    for t in range(2):
        pre = None
        for a in range(3):
            for b in range(3):
                window = wide[t + a, b : b + 4].reshape(256, 768)
                term = dot(window, weight[a, b].reshape(768, 128))
                pre = term if pre is None else pre + term
        sigm = jax.nn.sigmoid(pre)
        grad = cot[t].reshape(256, 128).astype(F32)
        slope[t] = (grad * sigm * (1.0 + pre * (1.0 - sigm))).astype(BF16).reshape(4, 64, 128)


def grads_body(
    where, slope, later, top, bottom, ltop, lbottom, weight, taps, before, btop, wide,
    lat_grad, own, send, gathered, rim, btaps, stage,
):
    seg = where[0]
    core = where[1]

    @pl.when(seg == 0)
    def _():
        for f in range(4):
            mid = slope if f < 2 else later
            up = top if f < 2 else ltop
            down = bottom if f < 2 else lbottom
            i = f % 2

            def lay(row):
                left, same, right = neighbour_cols(row)
                return jnp.concatenate([right, same, left], axis=1)

            rim[f, 0] = lay(up[i, 0])
            rim[f, 5] = lay(down[i, 0])
            for r in range(4):
                rim[f, r + 1] = lay(mid[i, r])
        fill_clip(stage, before, btop, btaps, 2)
        grads = []
        for t in range(2):
            total = None
            for a in range(3):
                for b in range(3):
                    window = rim[t + 2 - a, 2 - b : 6 - b].reshape(256, 384)
                    side = jnp.concatenate([weight[a, b, c] for c in range(3)], axis=1)
                    term = dot_nt(window, side)
                    total = term if total is None else total + term
            grad = total.astype(BF16)
            lat_grad[t] = grad.reshape(4, 64, 256)
            grads.append(grad)
        for a in range(3):
            for b in range(3):
                total = None
                for t in range(2):
                    f = 2 * t + a
                    rows = clip_im2col(btaps, f, b) if f < 2 else clip_im2col(taps, f - 2, b)
                    term = dot_tn(rows, grads[t])
                    total = term if total is None else total + term
                for c in range(3):
                    tap = (a * 3 + b) * 3 + c
                    for j in range(2):
                        gathered[pl.ds(tap * 256 + j, 128, stride=2), :] = total[
                            c * 128 : (c + 1) * 128, j * 128 : (j + 1) * 128
                        ]

    @pl.when(seg != 0)
    def _():
        lat_grad[...] = jnp.zeros(lat_grad.shape, BF16)
        for a in range(3):
            for b in range(3):
                total = None
                for t in range(2):
                    window = wide[t + a, b : b + 4].reshape(256, 768)
                    term = dot_tn(window, slope[t].reshape(256, 128))
                    total = term if total is None else total + term
                start = (a * 3 + b) * 768
                gathered[start : start + 768, :] = total

    half = own.shape[0]
    own[...] = gathered[pl.ds(pl.multiple_of(core * half, 8), half), :]
    send[...] = gathered[pl.ds(pl.multiple_of((1 - core) * half, 8), half), :].astype(BF16)


def part_of(ref, start, chunk, rows):
    return ref[pl.ds(pl.multiple_of(start + chunk * rows, 8), rows), :]


def halves_body(where, own, got, a_own, a1, a2, a3, b_own, b1, b2, b3, held):
    held[...] = own[...] + got[...].astype(F32)
    for start, at, mine, outs in ((0, where[0], a_own, (a1, a2, a3)), (1728, where[1], b_own, (b1, b2, b3))):
        mine[...] = part_of(held, start, at, 432)
        for k, out in enumerate(outs):
            out[...] = part_of(held, start, (at + k + 1) % 4, 432).astype(BF16)


def second_body(
    where, a_own, ra1, ra2, ra3, b_own, rb1, rb2, rb3, oa, a1, a2, a3, ob, b1, b2, b3, held
):
    held[...] = jnp.zeros(held.shape, F32)
    for start, at, own, got, mine, outs in (
        (0, where[1], a_own, (ra1, ra2, ra3), oa, (a1, a2, a3)),
        (448, where[0], b_own, (rb1, rb2, rb3), ob, (b1, b2, b3)),
    ):
        total = own[...]
        for one in got:
            total = total + one[...].astype(F32)
        held[start : start + 432, :] = total
        mine[...] = part_of(held, start, at, 112)
        for k, out in enumerate(outs):
            out[...] = part_of(held, start, (at + k + 1) % 4, 112)


def third_body(where, a_own, ra1, ra2, ra3, b_own, rb1, rb2, rb3, mine, s1, s2, s3, held):
    held[0:112, :] = a_own[...] + ra1[...] + ra2[...] + ra3[...]
    held[112:224, :] = b_own[...] + rb1[...] + rb2[...] + rb3[...]
    at = where[2]
    mine[...] = part_of(held, 0, at, 56)
    for k, out in enumerate((s1, s2, s3)):
        out[...] = part_of(held, 0, (at + k + 1) % 4, 56)


def fourth_body(own, r1, r2, r3, total):
    total[...] = own[...] + r1[...] + r2[...] + r3[...]


def put(ref, start, at, rows, pieces):
    for k, piece in enumerate(pieces):
        spot = pl.multiple_of(start + (at + 4 - k) % 4 * rows, 8)
        ref[pl.ds(spot, rows), :] = piece[...].astype(ref.dtype)


def fifth_body(where, own, r1, r2, r3, a, b, held):
    put(held, 0, where[2], 56, (own, r1, r2, r3))
    a[...] = held[0:112, :].astype(BF16)
    b[...] = held[112:224, :].astype(BF16)


def sixth_body(where, a, ra1, ra2, ra3, b, rb1, rb2, rb3, a_out, b_out, held):
    put(held, 0, where[1], 112, (a, ra1, ra2, ra3))
    put(held, 448, where[0], 112, (b, rb1, rb2, rb3))
    a_out[...] = held[0:432, :]
    b_out[...] = held[448 : 448 + 432, :]


def seventh_body(where, a, ra1, ra2, ra3, b, rb1, rb2, rb3, half):
    for start, at, pieces in ((0, where[0], (a, ra1, ra2, ra3)), (1728, where[1], (b, rb1, rb2, rb3))):
        put(half, start, at, 432, pieces)


def moved(array, axis, pairs):
    return lax.ppermute(array, axis, pairs)


def along_x(array, k):
    return moved(array, "tm", [(i, (i + 4 * k) % 16) for i in range(16)])


def along_z(array, k):
    return moved(array, "tm", [(i, i // 4 * 4 + (i + k) % 4) for i in range(16)])


def along_y(array, k):
    return moved(array, "space", [(i, (i + 2 * k) % 8) for i in range(8)])


def to_core(array):
    return moved(array, "space", [(i, i ^ 1) for i in range(8)])


def shifted(array, by_tm, by_space):
    frames = lax.axis_size("tm")
    rows = lax.axis_size("space")
    pairs = [
        (t * rows + s, (t + by_tm) * rows + s + by_space)
        for t in range(frames)
        for s in range(rows)
        if 0 <= t + by_tm < frames and 0 <= s + by_space < rows
    ]
    return moved(array, ("tm", "space"), pairs)


def summed(own, send, spots):
    rows = lambda n, dtype: shape((n, 128), dtype)
    got = to_core(send)
    outs = [rows(432, F32)] + [rows(432, BF16)] * 3
    a, a1, a2, a3, b, b1, b2, b3 = on_chip(
        halves_body, outs + outs, "halves", 1, [pltpu.VMEM((3456, 128), F32)]
    )(spots, own, got)
    ra = [along_x(v, k) for k, v in ((1, a1), (3, a3), (2, a2))]
    rb = [along_y(v, k) for k, v in ((1, b1), (3, b3), (2, b2))]
    outs = [rows(112, F32)] * 4
    a, a1, a2, a3, b, b1, b2, b3 = on_chip(
        second_body, outs + outs, "second", 1, [pltpu.VMEM((896, 128), F32)]
    )(spots, a, *ra, b, *rb)
    ra = [along_y(v, k) for k, v in ((1, a1), (3, a3), (2, a2))]
    rb = [along_x(v, k) for k, v in ((1, b1), (3, b3), (2, b2))]
    own, s1, s2, s3 = on_chip(
        third_body, [rows(56, F32)] * 4, "third", 1, [pltpu.VMEM((224, 128), F32)]
    )(spots, a, *ra, b, *rb)
    got = [along_z(v, k) for k, v in ((1, s1), (3, s3), (2, s2))]
    (total,) = on_chip(fourth_body, [rows(56, F32)], "fourth")(own, *got)
    got = [along_z(total, k) for k in (1, 2, 3)]
    a, b = on_chip(
        fifth_body, [rows(112, BF16)] * 2, "fifth", 1, [pltpu.VMEM((224, 128), F32)]
    )(spots, total, *got)
    ra = [along_y(a, k) for k in (1, 2, 3)]
    rb = [along_x(b, k) for k in (1, 2, 3)]
    a, b = on_chip(
        sixth_body, [rows(432, BF16)] * 2, "sixth", 1, [pltpu.VMEM((896, 128), BF16)]
    )(spots, a, *ra, b, *rb)
    ra = [along_x(a, k) for k in (1, 2, 3)]
    rb = [along_y(b, k) for k in (1, 2, 3)]
    (half,) = on_chip(seventh_body, [rows(3456, BF16)], "seventh", 1)(spots, a, *ra, b, *rb)
    return half, to_core(half)


def on_device(clip_frames, enc_weight, dec_weight, out_grad):
    seg = lax.axis_index("segment")
    tm = lax.axis_index("tm")
    space = lax.axis_index("space")
    core = space % 2
    spots = jnp.stack([tm // 4, space // 2, tm % 4])

    above = shifted(clip_frames[:, 7:8], 0, 1)
    lat1, part, own0, taps = on_chip(
        encode_body,
        [
            shape((4, 64, 256), BF16),
            shape((4, 64, 256), PART),
            shape((4, 64, 256), F32),
            shape((4, 9, 64, 384), BF16),
        ],
        "encode",
        scratch=[pltpu.VMEM((136, 128), F32)],
    )(clip_frames, above, enc_weight)

    def halo(lat):
        return (
            shifted(lat, 1, 0),
            shifted(lat[3:4], 0, 1),
            shifted(lat[0:1], 0, -1),
            shifted(lat[3:4], 1, 1),
            shifted(lat[0:1], 1, -1),
        )

    part = shifted(part, 1, 0)
    p1, t1, b1, pt1, pb1 = halo(lat1)
    lat0 = (own0 + part.astype(F32)).astype(BF16)
    p0, t0, b0, pt0, pb0 = halo(lat0)
    slope, wide = on_chip(
        decode_body, [shape((2, 4, 64, 128), BF16), shape((4, 6, 64, 768), BF16)], "decode"
    )(p0, p1, lat0, lat1, pt0, pt1, t0, t1, pb0, pb1, b0, b1, dec_weight, out_grad)

    clip_late, above_late, _ = lax.optimization_barrier((clip_frames[2:4], above[2:4], p0))
    before = shifted(clip_late, 1, 0)
    before_top = shifted(above_late, 1, 0)
    later = shifted(slope, -1, 0)
    top = shifted(slope[:, 3:4], 0, 1)
    bottom = shifted(slope[:, 0:1], 0, -1)
    later_top = shifted(slope[:, 3:4], -1, 1)
    later_bottom = shifted(slope[:, 0:1], -1, -1)
    lat_grad, own, send = on_chip(
        grads_body,
        [
            shape((2, 4, 64, 256), BF16),
            shape((3456, 128), F32),
            shape((3456, 128), BF16),
        ],
        "grads",
        1,
        [
            pltpu.VMEM((6912, 128), F32),
            pltpu.VMEM((4, 6, 64, 384), BF16),
            pltpu.VMEM((2, 9, 64, 384), BF16),
            pltpu.VMEM((136, 128), F32),
        ],
    )(
        jnp.stack([seg, core]),
        slope, later, top, bottom, later_top, later_bottom, dec_weight, taps, before, before_top, wide,
    )
    latent = jnp.stack([lat0, lat1])
    latent_pair = jnp.where(seg == 0, lat_grad, latent)[None]
    half, other = summed(own, send, spots)
    whole = jnp.where(core == 0, jnp.stack([half, other]), jnp.stack([other, half]))
    weight_grads = whole.reshape(27, 32768).astype(F32) * (1.0 / math.sqrt(32 * 32 * 64))
    return latent_pair, weight_grads[None]


def solution(mesh):
    placed = (P("tm", "space", None, None), P(), P(), P("tm", "space", None, None))
    return jax.shard_map(
        on_device,
        mesh=mesh,
        in_specs=placed,
        out_specs=(P("segment", "tm", "space", None, None), P("segment", None, None)),
        check_vma=False,
    )
```

```python
import math

import jax
import jax.numpy as jnp
from jax import lax
from jax.experimental import pallas as pl
from jax.experimental.pallas import tpu as pltpu
from jax.sharding import Mesh, PartitionSpec as P

F32 = jnp.float32
BF16 = jnp.bfloat16
PART = BF16
MIB = 1024 * 1024


def shape(dims, dtype):
    return jax.ShapeDtypeStruct(dims, dtype)


def on_chip(body, outs, name, smem=0, scratch=(), grant=10):
    def call(*args):
        specs = [pl.BlockSpec(memory_space=pltpu.SMEM)] * smem
        specs += [pl.BlockSpec(memory_space=pltpu.VMEM)] * (len(args) - smem)
        return pl.pallas_call(
            body,
            out_shape=outs,
            in_specs=specs,
            out_specs=[pl.BlockSpec(memory_space=pltpu.VMEM)] * len(outs),
            scratch_shapes=list(scratch),
            name=name,
            compiler_params=pltpu.CompilerParams(vmem_limit_bytes=grant * MIB),
        )(*args)

    return call


def dot(left, right):
    return jnp.dot(left, right, preferred_element_type=F32)


def dot_tn(left, right):
    return lax.dot_general(left, right, (((0,), (0,)), ((), ())), preferred_element_type=F32)


def dot_nt(left, right):
    return lax.dot_general(left, right, (((1,), (1,)), ((), ())), preferred_element_type=F32)


def clip_windows(row, stage):
    stage[8:136, :] = row.astype(F32)
    before = stage[pl.ds(7, 64, stride=2), :]
    here = stage[pl.ds(8, 64, stride=2), :]
    after = stage[pl.ds(9, 64, stride=2), :]
    return jnp.concatenate([before, here, after], axis=1).astype(BF16)


def neighbour_cols(row):
    wide = row.astype(F32)
    place = lax.broadcasted_iota(jnp.int32, wide.shape, 0)
    last = wide.shape[0] - 1
    before = jnp.where(place == 0, 0.0, pltpu.roll(wide, 1, 0)).astype(BF16)
    after = jnp.where(place == last, 0.0, pltpu.roll(wide, last, 0)).astype(BF16)
    return before, row, after


def fill_clip(stage, src, top, dst, frames):
    stage[0:8, :] = jnp.zeros((8, stage.shape[1]), F32)
    for f in range(frames):
        dst[f, 0] = clip_windows(top[f, 0], stage)

        def one(r, carry, f=f):
            dst[f, r + 1] = clip_windows(src[f, r], stage)
            return carry

        lax.fori_loop(0, 8, one, 0)


def clip_im2col(taps, f, b):
    return jnp.concatenate([taps[f, 2 * h + b] for h in range(4)], axis=0)


def encode_body(clip, top, weight, lat1, part, own0, tail, taps, stage):
    fill_clip(stage, clip, top, taps, 4)

    def conv(f, a):
        total = None
        for b in range(3):
            term = dot(clip_im2col(taps, f, b), weight[a, b].reshape(384, 256))
            total = term if total is None else total + term
        return total

    part[...] = (conv(2, 0) + conv(3, 1)).astype(part.dtype).reshape(4, 64, 256)
    lat1[...] = (conv(0, 0) + conv(1, 1) + conv(2, 2)).astype(BF16).reshape(4, 64, 256)
    own0[...] = conv(0, 2).reshape(4, 64, 256)
    tail[:, 0:1] = top[2:4]
    tail[:, 1:9] = clip[2:4]


def decode_body(lat, top, bottom, weight, own, part, wide):
    for f in range(2):
        wide[f, 0] = jnp.concatenate(neighbour_cols(top[f, 0]), axis=1)
        wide[f, 5] = jnp.concatenate(neighbour_cols(bottom[f, 0]), axis=1)

        def one(r, carry, f=f):
            wide[f, r + 1] = jnp.concatenate(neighbour_cols(lat[f, r]), axis=1)
            return carry

        lax.fori_loop(0, 4, one, 0)

    def conv(f, a):
        total = None
        for b in range(3):
            window = wide[f, b : b + 4].reshape(256, 768)
            term = dot(window, weight[a, b].reshape(768, 128))
            total = term if total is None else total + term
        return total

    part[0] = (conv(0, 0) + conv(1, 1)).astype(part.dtype).reshape(4, 64, 128)
    part[1] = conv(1, 0).astype(part.dtype).reshape(4, 64, 128)
    own[0] = conv(0, 2).reshape(4, 64, 128)
    own[1] = (conv(0, 1) + conv(1, 2)).reshape(4, 64, 128)


def slope_body(own, part, cot, slope):
    pre = own[...] + part[...].astype(F32)
    sigm = jax.nn.sigmoid(pre)
    slope[...] = (cot[...].astype(F32) * sigm * (1.0 + pre * (1.0 - sigm))).astype(BF16)


def grads_body(
    where, slope, later, weight, taps, tail, wide, lat_grad, own, send, gathered, rim, btaps, stage
):
    seg = where[0]
    core = where[1]

    @pl.when(seg == 0)
    def _():
        for f in range(4):
            src = slope if f < 2 else later
            for r in range(6):
                left, same, right = neighbour_cols(src[f % 2, r])
                rim[f, r] = jnp.concatenate([right, same, left], axis=1)
        fill_clip(stage, tail.at[:, 1:9], tail, btaps, 2)
        grads = []
        for t in range(2):
            total = None
            for a in range(3):
                for b in range(3):
                    window = rim[t + 2 - a, 2 - b : 6 - b].reshape(256, 384)
                    side = jnp.concatenate([weight[a, b, c] for c in range(3)], axis=1)
                    term = dot_nt(window, side)
                    total = term if total is None else total + term
            grad = total.astype(BF16)
            lat_grad[t] = grad.reshape(4, 64, 256)
            grads.append(grad)
        for a in range(3):
            for b in range(3):
                total = None
                for t in range(2):
                    f = 2 * t + a
                    rows = clip_im2col(btaps, f, b) if f < 2 else clip_im2col(taps, f - 2, b)
                    term = dot_tn(rows, grads[t])
                    total = term if total is None else total + term
                for c in range(3):
                    tap = (a * 3 + b) * 3 + c
                    for j in range(2):
                        gathered[pl.ds(tap * 256 + j, 128, stride=2), :] = total[
                            c * 128 : (c + 1) * 128, j * 128 : (j + 1) * 128
                        ]

    @pl.when(seg != 0)
    def _():
        lat_grad[...] = jnp.zeros(lat_grad.shape, BF16)
        for a in range(3):
            for b in range(3):
                total = None
                for f in range(2):
                    t = f + 2 - a
                    cells = (slope if t < 2 else later)[t % 2, 1:5].reshape(256, 128)
                    term = dot_tn(wide[f, b : b + 4].reshape(256, 768), cells)
                    total = term if total is None else total + term
                start = (a * 3 + b) * 768
                gathered[start : start + 768, :] = total

    half = own.shape[0]
    own[...] = gathered[pl.ds(pl.multiple_of(core * half, 8), half), :]
    send[...] = gathered[pl.ds(pl.multiple_of((1 - core) * half, 8), half), :].astype(BF16)


def halves_body(own, got, spread):
    for j in range(16):
        rows = slice(216 * j, 216 * (j + 1))
        spread[j] = (own[rows, :] + got[rows, :].astype(F32)).astype(BF16)


def second_body(got, spread, held):
    total = got[0].astype(F32)
    for j in range(1, 16):
        total = total + got[j].astype(F32)
    held[0:216, :] = total
    held[216:224, :] = jnp.zeros((8, 128), F32)
    for j in range(4):
        spread[j] = held[56 * j : 56 * (j + 1), :]


def third_body(got, spread):
    total = got[0] + got[1] + got[2] + got[3]
    for j in range(4):
        spread[j] = total


def fourth_body(got, spread, held):
    for j in range(4):
        held[56 * j : 56 * (j + 1), :] = got[j]
    total = held[0:216, :].astype(BF16)
    for j in range(16):
        spread[j] = total


def exchanged(array, axes):
    return lax.all_to_all(array, axes, 0, 0, tiled=True)


def to_core(array):
    return lax.ppermute(array, "c", [(0, 1), (1, 0)])


def by_frames(array, by):
    pairs = [(i, i + by) for i in range(16) if 0 <= i + by < 16]
    return lax.ppermute(array, ("x", "z"), pairs)


def by_rows(array, by):
    pairs = [(i, i + by) for i in range(8) if 0 <= i + by < 8]
    return lax.ppermute(array, ("y", "c"), pairs)


def summed(own, send):
    got = to_core(send)
    (wide,) = on_chip(halves_body, [shape((16, 216, 128), BF16)], "halves")(own, got)
    (thin,) = on_chip(
        second_body, [shape((4, 56, 128), F32)], "second", scratch=[pltpu.VMEM((224, 128), F32)]
    )(exchanged(wide, ("x", "y")))
    (thin,) = on_chip(third_body, [shape((4, 56, 128), F32)], "third")(exchanged(thin, "z"))
    (wide,) = on_chip(
        fourth_body, [shape((16, 216, 128), BF16)], "fourth", scratch=[pltpu.VMEM((224, 128), F32)]
    )(exchanged(thin, "z"))
    half = exchanged(wide, ("x", "y")).reshape(3456, 128)
    return half, to_core(half)


def on_device(clip_frames, enc_weight, dec_weight, out_grad):
    seg = lax.axis_index("segment")
    core = lax.axis_index("c")

    above = by_rows(clip_frames[:, 7:8], 1)
    lat1, part, own0, tail, taps = on_chip(
        encode_body,
        [
            shape((4, 64, 256), BF16),
            shape((4, 64, 256), PART),
            shape((4, 64, 256), F32),
            shape((2, 9, 128, 128), BF16),
            shape((4, 9, 64, 384), BF16),
        ],
        "encode",
        scratch=[pltpu.VMEM((136, 128), F32)],
        grant=16,
    )(clip_frames, above, enc_weight)
    part = by_frames(part, 1)
    latent = jnp.stack([(own0 + part.astype(F32)).astype(BF16), lat1])
    top = by_rows(latent[:, 3:4], 1)
    bottom = by_rows(latent[:, 0:1], -1)
    own, part, wide = on_chip(
        decode_body,
        [
            shape((2, 4, 64, 128), F32),
            shape((2, 4, 64, 128), PART),
            shape((2, 6, 64, 768), BF16),
        ],
        "decode",
        grant=12,
    )(latent, top, bottom, dec_weight)
    part = by_frames(part, 1)
    tail, _ = lax.optimization_barrier((tail, part))
    tail = lax.ppermute(tail, ("segment", "x", "z"), [(16 + t - 1, t) for t in range(1, 16)])
    (slope,) = on_chip(slope_body, [shape((2, 4, 64, 128), BF16)], "slope")(own, part, out_grad)
    top = by_rows(slope[:, 3:4], 1)
    bottom = by_rows(slope[:, 0:1], -1)
    slope = jnp.concatenate([top, slope, bottom], axis=1)
    later = by_frames(slope, -1)
    lat_grad, own, send = on_chip(
        grads_body,
        [
            shape((2, 4, 64, 256), BF16),
            shape((3456, 128), F32),
            shape((3456, 128), BF16),
        ],
        "grads",
        1,
        [
            pltpu.VMEM((6912, 128), F32),
            pltpu.VMEM((4, 6, 64, 384), BF16),
            pltpu.VMEM((2, 9, 64, 384), BF16),
            pltpu.VMEM((136, 128), F32),
        ],
        24,
    )(jnp.stack([seg, core]), slope, later, dec_weight, taps, tail, wide)
    latent_pair = jnp.where(seg == 0, lat_grad, latent)[None]
    half, other = summed(own, send)
    whole = jnp.where(core == 0, jnp.stack([half, other]), jnp.stack([other, half]))
    weight_grads = whole.reshape(27, 32768).astype(F32) * (1.0 / math.sqrt(32 * 32 * 64))
    return latent_pair, weight_grads[None]


def solution(mesh):
    fine = Mesh(mesh.devices.reshape(2, 4, 4, 4, 2), ("segment", "x", "z", "y", "c"))
    cells = P(("x", "z"), ("y", "c"), None, None)
    return jax.shard_map(
        on_device,
        mesh=fine,
        in_specs=(cells, P(), P(), cells),
        out_specs=(P("segment", ("x", "z"), ("y", "c"), None, None), P("segment", None, None)),
        check_vma=False,
    )
```

```python
import math

import jax
import jax.numpy as jnp
from jax import lax
from jax.experimental import pallas as pl
from jax.experimental.pallas import tpu as pltpu
from jax.sharding import Mesh, PartitionSpec as P

F32 = jnp.float32
BF16 = jnp.bfloat16
PART = BF16
MIB = 1024 * 1024


def shape(dims, dtype):
    return jax.ShapeDtypeStruct(dims, dtype)


def on_chip(body, outs, name, smem=0, scratch=(), grant=10):
    def call(*args):
        specs = [pl.BlockSpec(memory_space=pltpu.SMEM)] * smem
        specs += [pl.BlockSpec(memory_space=pltpu.VMEM)] * (len(args) - smem)
        return pl.pallas_call(
            body,
            out_shape=outs,
            in_specs=specs,
            out_specs=[pl.BlockSpec(memory_space=pltpu.VMEM)] * len(outs),
            scratch_shapes=list(scratch),
            name=name,
            compiler_params=pltpu.CompilerParams(vmem_limit_bytes=grant * MIB),
        )(*args)

    return call


def dot(left, right):
    return jnp.dot(left, right, preferred_element_type=F32)


def dot_tn(left, right):
    return lax.dot_general(left, right, (((0,), (0,)), ((), ())), preferred_element_type=F32)


def dot_nt(left, right):
    return lax.dot_general(left, right, (((1,), (1,)), ((), ())), preferred_element_type=F32)


def clip_windows(row, stage):
    stage[8:136, :] = row.astype(F32)
    before = stage[pl.ds(7, 64, stride=2), :]
    here = stage[pl.ds(8, 64, stride=2), :]
    after = stage[pl.ds(9, 64, stride=2), :]
    return jnp.concatenate([before, here, after], axis=1).astype(BF16)


def neighbour_cols(row):
    wide = row.astype(F32)
    place = lax.broadcasted_iota(jnp.int32, wide.shape, 0)
    last = wide.shape[0] - 1
    before = jnp.where(place == 0, 0.0, pltpu.roll(wide, 1, 0)).astype(BF16)
    after = jnp.where(place == last, 0.0, pltpu.roll(wide, last, 0)).astype(BF16)
    return before, row, after


def fill_clip(stage, src, top, dst, frames):
    stage[0:8, :] = jnp.zeros((8, stage.shape[1]), F32)
    for f in range(frames):
        dst[f, 0] = clip_windows(top[f, 0], stage)

        def one(r, carry, f=f):
            dst[f, r + 1] = clip_windows(src[f, r], stage)
            return carry

        lax.fori_loop(0, 8, one, 0)


def clip_im2col(taps, f, b):
    return jnp.concatenate([taps[f, 2 * h + b] for h in range(4)], axis=0)


def encode_body(clip, top, weight, cot, lat1, part, own0, tail, cot_down, cot_up, taps, stage):
    fill_clip(stage, clip, top, taps, 4)

    def conv(f, a):
        total = None
        for b in range(3):
            term = dot(clip_im2col(taps, f, b), weight[a, b].reshape(384, 256))
            total = term if total is None else total + term
        return total

    part[...] = (conv(2, 0) + conv(3, 1)).astype(part.dtype).reshape(4, 64, 256)
    lat1[...] = (conv(0, 0) + conv(1, 1) + conv(2, 2)).astype(BF16).reshape(4, 64, 256)
    own0[...] = conv(0, 2).reshape(4, 64, 256)
    tail[:, 0:1] = top[2:4]
    tail[:, 1:9] = clip[2:4]
    cot_down[...] = cot[:, 3:4]
    cot_up[...] = cot[:, 0:1]


def join_body(own0, part, lat1, lat, down, up):
    lat[0] = (own0[...] + part[...].astype(F32)).astype(BF16)
    lat[1] = lat1[...]
    down[...] = lat[:, 2:4]
    up[...] = lat[:, 0:2]


def fill_latent(lat, top, bottom, wide):
    for f in range(2):
        for r in range(2):
            wide[f, r] = jnp.concatenate(neighbour_cols(top[f, r]), axis=1)
            wide[f, 6 + r] = jnp.concatenate(neighbour_cols(bottom[f, r]), axis=1)

        def one(r, carry, f=f):
            wide[f, r + 2] = jnp.concatenate(neighbour_cols(lat[f, r]), axis=1)
            return carry

        lax.fori_loop(0, 4, one, 0)


def decode_body(lat, top, bottom, weight, own, part, wide):
    fill_latent(lat, top, bottom, wide)

    def conv(f, a):
        total = None
        for b in range(3):
            window = wide[f, b : b + 6].reshape(384, 768)
            term = dot(window, weight[a, b].reshape(768, 128))
            total = term if total is None else total + term
        return total

    part[0] = (conv(0, 0) + conv(1, 1)).astype(part.dtype).reshape(6, 64, 128)
    part[1] = conv(1, 0).astype(part.dtype).reshape(6, 64, 128)
    own[0] = conv(0, 2).reshape(6, 64, 128)
    own[1] = (conv(0, 1) + conv(1, 2)).reshape(6, 64, 128)


def slope_body(own, part, cot, top, bottom, slope):
    def rows(at, grad):
        pre = own[:, at] + part[:, at].astype(F32)
        sigm = jax.nn.sigmoid(pre)
        slope[:, at] = (grad.astype(F32) * sigm * (1.0 + pre * (1.0 - sigm))).astype(BF16)

    rows(slice(0, 1), top[...])
    rows(slice(1, 5), cot[...])
    rows(slice(5, 6), bottom[...])


def grads_body(
    seg_at, core_at, slope, later, weight, taps, tail, lat, top, bottom,
    lat_grad, own, send, gathered, rim, btaps, wide, stage,
):
    seg = seg_at[0]
    core = core_at[0]

    @pl.when(seg == 0)
    def _():
        for f in range(4):
            src = slope if f < 2 else later
            for r in range(6):
                left, same, right = neighbour_cols(src[f % 2, r])
                rim[f, r] = jnp.concatenate([right, same, left], axis=1)
        fill_clip(stage, tail.at[:, 1:9], tail, btaps, 2)
        grads = []
        for t in range(2):
            total = None
            for a in range(3):
                for b in range(3):
                    window = rim[t + 2 - a, 2 - b : 6 - b].reshape(256, 384)
                    side = jnp.concatenate([weight[a, b, c] for c in range(3)], axis=1)
                    term = dot_nt(window, side)
                    total = term if total is None else total + term
            grad = total.astype(BF16)
            lat_grad[t] = grad.reshape(4, 64, 256)
            grads.append(grad)
        for a in range(3):
            for b in range(3):
                total = None
                for t in range(2):
                    f = 2 * t + a
                    rows = clip_im2col(btaps, f, b) if f < 2 else clip_im2col(taps, f - 2, b)
                    term = dot_tn(rows, grads[t])
                    total = term if total is None else total + term
                for c in range(3):
                    tap = (a * 3 + b) * 3 + c
                    for j in range(2):
                        gathered[pl.ds(tap * 256 + j, 128, stride=2), :] = total[
                            c * 128 : (c + 1) * 128, j * 128 : (j + 1) * 128
                        ]

    @pl.when(seg != 0)
    def _():
        lat_grad[...] = jnp.zeros(lat_grad.shape, BF16)
        fill_latent(lat, top, bottom, wide)
        for a in range(3):
            for b in range(3):
                total = None
                for f in range(2):
                    t = f + 2 - a
                    cells = (slope if t < 2 else later)[t % 2, 1:5].reshape(256, 128)
                    term = dot_tn(wide[f, b + 1 : b + 5].reshape(256, 768), cells)
                    total = term if total is None else total + term
                start = (a * 3 + b) * 768
                gathered[start : start + 768, :] = total

    half = own.shape[0]
    own[...] = gathered[pl.ds(pl.multiple_of(core * half, 8), half), :]
    send[...] = gathered[pl.ds(pl.multiple_of((1 - core) * half, 8), half), :].astype(BF16)


def halves_body(own, got, spread):
    for j in range(16):
        rows = slice(216 * j, 216 * (j + 1))
        spread[j] = (own[rows, :] + got[rows, :].astype(F32)).astype(BF16)


def second_body(got, spread):
    total = got[0].astype(F32)
    for j in range(1, 16):
        total = total + got[j].astype(F32)
    for j in range(4):
        spread[j] = total.astype(BF16)


def third_body(got, spread):
    total = got[0].astype(F32)
    for j in range(1, 4):
        total = total + got[j].astype(F32)
    for j in range(16):
        spread[j] = total.astype(BF16)


def exchanged(array, axes):
    return lax.all_to_all(array, axes, 0, 0, tiled=True)


def to_core(array):
    return lax.ppermute(array, "c", [(0, 1), (1, 0)])


def by_frames(array, by):
    pairs = [(i, i + by) for i in range(16) if 0 <= i + by < 16]
    return lax.ppermute(array, ("x", "z"), pairs)


def by_rows(array, by):
    pairs = [(i, i + by) for i in range(8) if 0 <= i + by < 8]
    return lax.ppermute(array, ("y", "c"), pairs)


def summed(own, send):
    got = to_core(send)
    (wide,) = on_chip(halves_body, [shape((16, 216, 128), BF16)], "halves")(own, got)
    (thin,) = on_chip(second_body, [shape((4, 216, 128), BF16)], "second")(
        exchanged(wide, ("x", "y"))
    )
    (wide,) = on_chip(third_body, [shape((16, 216, 128), BF16)], "third")(exchanged(thin, "z"))
    half = exchanged(wide, ("x", "y")).reshape(3456, 128)
    return half, to_core(half)


def on_device(clip_frames, enc_weight, dec_weight, out_grad):
    seg = lax.axis_index("segment")
    core = lax.axis_index("c")

    above = by_rows(clip_frames[:, 7:8], 1)
    lat1, part, own0, tail, cot_down, cot_up, taps = on_chip(
        encode_body,
        [
            shape((4, 64, 256), BF16),
            shape((4, 64, 256), PART),
            shape((4, 64, 256), F32),
            shape((2, 9, 128, 128), BF16),
            shape((2, 1, 64, 128), BF16),
            shape((2, 1, 64, 128), BF16),
            shape((4, 9, 64, 384), BF16),
        ],
        "encode",
        scratch=[pltpu.VMEM((136, 128), F32)],
        grant=16,
    )(clip_frames, above, enc_weight, out_grad)
    part = by_frames(part, 1)
    cot_top = by_rows(cot_down, 1)
    cot_bottom = by_rows(cot_up, -1)
    part, cot_top, cot_bottom = lax.optimization_barrier((part, cot_top, cot_bottom))
    latent, down, up = on_chip(
        join_body,
        [
            shape((2, 4, 64, 256), BF16),
            shape((2, 2, 64, 256), BF16),
            shape((2, 2, 64, 256), BF16),
        ],
        "join",
    )(own0, part, lat1)
    top = by_rows(down, 1)
    bottom = by_rows(up, -1)
    own, part = on_chip(
        decode_body,
        [shape((2, 6, 64, 128), F32), shape((2, 6, 64, 128), PART)],
        "decode",
        scratch=[pltpu.VMEM((2, 8, 64, 768), BF16)],
        grant=14,
    )(latent, top, bottom, dec_weight)
    part = by_frames(part, 1)
    tail, _ = lax.optimization_barrier((tail, part))
    tail = lax.ppermute(tail, ("segment", "x", "z"), [(16 + t - 1, t) for t in range(1, 16)])
    (slope,) = on_chip(slope_body, [shape((2, 6, 64, 128), BF16)], "slope")(
        own, part, out_grad, cot_top, cot_bottom
    )
    later = by_frames(slope, -1)
    lat_grad, own, send = on_chip(
        grads_body,
        [
            shape((2, 4, 64, 256), BF16),
            shape((3456, 128), F32),
            shape((3456, 128), BF16),
        ],
        "grads",
        2,
        [
            pltpu.VMEM((6912, 128), F32),
            pltpu.VMEM((4, 6, 64, 384), BF16),
            pltpu.VMEM((2, 9, 64, 384), BF16),
            pltpu.VMEM((2, 8, 64, 768), BF16),
            pltpu.VMEM((136, 128), F32),
        ],
        26,
    )(seg.reshape(1), core.reshape(1), slope, later, dec_weight, taps, tail, latent, top, bottom)
    latent_pair = jnp.where(seg == 0, lat_grad, latent)[None]
    half, other = summed(own, send)
    whole = jnp.where(core == 0, jnp.stack([half, other]), jnp.stack([other, half]))
    weight_grads = whole.reshape(27, 32768).astype(F32) * (1.0 / math.sqrt(32 * 32 * 64))
    return latent_pair, weight_grads[None]


def solution(mesh):
    fine = Mesh(mesh.devices.reshape(2, 4, 4, 4, 2), ("segment", "x", "z", "y", "c"))
    cells = P(("x", "z"), ("y", "c"), None, None)
    return jax.shard_map(
        on_device,
        mesh=fine,
        in_specs=(cells, P(), P(), cells),
        out_specs=(P("segment", ("x", "z"), ("y", "c"), None, None), P("segment", None, None)),
        check_vma=False,
    )
```

```python
import math

import jax
import jax.numpy as jnp
from jax import lax
from jax.experimental import pallas as pl
from jax.experimental.pallas import tpu as pltpu
from jax.sharding import Mesh, PartitionSpec as P

F32 = jnp.float32
BF16 = jnp.bfloat16
PART = BF16
MIB = 1024 * 1024


def shape(dims, dtype):
    return jax.ShapeDtypeStruct(dims, dtype)


def on_chip(body, outs, name, smem=0, scratch=(), grant=10):
    def call(*args):
        specs = [pl.BlockSpec(memory_space=pltpu.SMEM)] * smem
        specs += [pl.BlockSpec(memory_space=pltpu.VMEM)] * (len(args) - smem)
        return pl.pallas_call(
            body,
            out_shape=outs,
            in_specs=specs,
            out_specs=[pl.BlockSpec(memory_space=pltpu.VMEM)] * len(outs),
            scratch_shapes=list(scratch),
            name=name,
            compiler_params=pltpu.CompilerParams(vmem_limit_bytes=grant * MIB),
        )(*args)

    return call


def dot(left, right):
    return jnp.dot(left, right, preferred_element_type=F32)


def dot_tn(left, right):
    return lax.dot_general(left, right, (((0,), (0,)), ((), ())), preferred_element_type=F32)


def dot_nt(left, right):
    return lax.dot_general(left, right, (((1,), (1,)), ((), ())), preferred_element_type=F32)


def clip_windows(row, stage):
    stage[8:136, :] = row.astype(F32)
    before = stage[pl.ds(7, 64, stride=2), :]
    here = stage[pl.ds(8, 64, stride=2), :]
    after = stage[pl.ds(9, 64, stride=2), :]
    return jnp.concatenate([before, here, after], axis=1).astype(BF16)


def neighbour_cols(row):
    wide = row.astype(F32)
    place = lax.broadcasted_iota(jnp.int32, wide.shape, 0)
    last = wide.shape[0] - 1
    before = jnp.where(place == 0, 0.0, pltpu.roll(wide, 1, 0)).astype(BF16)
    after = jnp.where(place == last, 0.0, pltpu.roll(wide, last, 0)).astype(BF16)
    return before, row, after


def start_stage(stage):
    stage[0:8, :] = jnp.zeros((8, stage.shape[1]), F32)


def edge_body(clip, cot, down):
    down[0:4] = clip[:, 7]
    down[4, 0:64] = cot[0, 3]
    down[4, 64:128] = cot[1, 3]


def windows_body(clip, taps, stage):
    start_stage(stage)
    for f in range(4):

        def one(r, carry, f=f):
            taps[f, r] = clip_windows(clip[f, r], stage)
            return carry

        lax.fori_loop(0, 8, one, 0)


def clip_im2col(tops, taps, f, b):
    rows = [2 * h + b for h in range(4)]
    return jnp.concatenate([tops[f] if p == 0 else taps[f, p - 1] for p in rows], axis=0)


def encode_body(
    clip, taps, above, weight, cot, below, lat1, part, own0, tail, tops, rows6, stage
):
    start_stage(stage)
    for f in range(4):
        tops[f] = clip_windows(above[f], stage)

    def conv(f, a):
        total = None
        for b in range(3):
            term = dot(clip_im2col(tops, taps, f, b), weight[a, b].reshape(384, 256))
            total = term if total is None else total + term
        return total

    part[...] = (conv(2, 0) + conv(3, 1)).astype(part.dtype).reshape(4, 64, 256)
    lat1[...] = (conv(0, 0) + conv(1, 1) + conv(2, 2)).astype(BF16).reshape(4, 64, 256)
    own0[...] = conv(0, 2).reshape(4, 64, 256)
    tail[:, 0] = above[2:4]
    tail[:, 1:9] = clip[2:4]
    rows6[0, 0] = above[4, 0:64]
    rows6[1, 0] = above[4, 64:128]
    rows6[:, 1:5] = cot[...]
    rows6[:, 5:6] = below[...]


def join_body(own0, part, lat1, lat, down, up):
    lat[0] = (own0[...] + part[...].astype(F32)).astype(BF16)
    lat[1] = lat1[...]
    down[...] = lat[:, 2:4]
    up[...] = lat[:, 0:2]


def fill_latent(lat, top, bottom, wide):
    for f in range(2):
        for r in range(2):
            wide[f, r] = jnp.concatenate(neighbour_cols(top[f, r]), axis=1)
            wide[f, 6 + r] = jnp.concatenate(neighbour_cols(bottom[f, r]), axis=1)

        def one(r, carry, f=f):
            wide[f, r + 2] = jnp.concatenate(neighbour_cols(lat[f, r]), axis=1)
            return carry

        lax.fori_loop(0, 4, one, 0)


def decode_body(lat, top, bottom, weight, own, behind, part, wide):
    fill_latent(lat, top, bottom, wide)

    def conv(f, a):
        total = None
        for b in range(3):
            window = wide[f, b : b + 6].reshape(384, 768)
            term = dot(window, weight[a, b].reshape(768, 128))
            total = term if total is None else total + term
        return total

    part[0] = (conv(0, 0) + conv(1, 1)).astype(part.dtype).reshape(6, 64, 128)
    part[1] = conv(1, 0).astype(part.dtype).reshape(6, 64, 128)
    own[0] = conv(0, 2).reshape(6, 64, 128)
    own[1] = (conv(0, 1) + conv(1, 2)).reshape(6, 64, 128)
    behind[...] = own[...].astype(behind.dtype)


def turned_body(seg_at, tail, tops, taps, lat, top, bottom, turned, btops, btaps, wide, stage):
    seg = seg_at[0]

    @pl.when(seg == 0)
    def _():
        start_stage(stage)
        for f in range(2):
            btops[f] = clip_windows(tail[f, 0], stage)

            def one(r, carry, f=f):
                btaps[f, r] = clip_windows(tail[f, r + 1], stage)
                return carry

            lax.fori_loop(0, 8, one, 0)
        for f in range(5):
            for b in range(3):
                rows = clip_im2col(btops, btaps, f, b) if f < 2 else clip_im2col(tops, taps, f - 2, b)
                turned[f * 3 + b] = rows.T

    @pl.when(seg != 0)
    def _():
        fill_latent(lat, top, bottom, wide)
        for f in range(2):
            for b in range(3):
                flat = wide[f, b + 1 : b + 5].reshape(256, 768).T
                turned[(f * 3 + b) * 2] = flat[0:384]
                turned[(f * 3 + b) * 2 + 1] = flat[384:768]


def grads_body(
    seg_at, core_at, own_part, from_behind, gone, from_later, cot, later_cot, weight, turned,
    lat_grad, own, send, gathered, slopes, rim,
):
    seg = seg_at[0]
    core = core_at[0]

    def slope_of(pre, grad):
        sigm = jax.nn.sigmoid(pre)
        return (grad.astype(F32) * sigm * (1.0 + pre * (1.0 - sigm))).astype(BF16)

    slopes[0:2] = slope_of(own_part[...] + from_behind[...].astype(F32), cot[...])
    slopes[2:4] = slope_of(from_later[...].astype(F32) + gone[...].astype(F32), later_cot[...])

    @pl.when(seg == 0)
    def _():
        for f in range(4):
            for r in range(6):
                left, same, right = neighbour_cols(slopes[f, r])
                rim[f, r] = jnp.concatenate([right, same, left], axis=1)
        grads = []
        for t in range(2):
            total = None
            for a in range(3):
                for b in range(3):
                    window = rim[t + 2 - a, 2 - b : 6 - b].reshape(256, 384)
                    side = jnp.concatenate([weight[a, b, c] for c in range(3)], axis=1)
                    term = dot_nt(window, side)
                    total = term if total is None else total + term
            grad = total.astype(BF16)
            lat_grad[t] = grad.reshape(4, 64, 256)
            grads.append(grad)
        for a in range(3):
            for b in range(3):
                total = dot(turned[a * 3 + b], grads[0]) + dot(turned[(a + 2) * 3 + b], grads[1])
                for c in range(3):
                    tap = (a * 3 + b) * 3 + c
                    for j in range(2):
                        gathered[pl.ds(tap * 256 + j, 128, stride=2), :] = total[
                            c * 128 : (c + 1) * 128, j * 128 : (j + 1) * 128
                        ]

    @pl.when(seg != 0)
    def _():
        lat_grad[...] = jnp.zeros(lat_grad.shape, BF16)
        for a in range(3):
            for b in range(3):
                for i in range(2):
                    total = None
                    for f in range(2):
                        cells = slopes[f + 2 - a, 1:5].reshape(256, 128)
                        term = dot(turned[(f * 3 + b) * 2 + i], cells)
                        total = term if total is None else total + term
                    start = (a * 3 + b) * 768 + i * 384
                    gathered[start : start + 384, :] = total

    half = own.shape[0]
    own[...] = gathered[pl.ds(pl.multiple_of(core * half, 8), half), :]
    send[...] = gathered[pl.ds(pl.multiple_of((1 - core) * half, 8), half), :].astype(BF16)


def halves_body(own, got, spread):
    for j in range(16):
        rows = slice(216 * j, 216 * (j + 1))
        spread[j] = (own[rows, :] + got[rows, :].astype(F32)).astype(BF16)


def second_body(got, spread):
    total = got[0].astype(F32)
    for j in range(1, 16):
        total = total + got[j].astype(F32)
    for j in range(4):
        spread[j] = total.astype(BF16)


def third_body(got, spread):
    total = got[0].astype(F32)
    for j in range(1, 4):
        total = total + got[j].astype(F32)
    for j in range(16):
        spread[j] = total.astype(BF16)


def exchanged(array, axes):
    return lax.all_to_all(array, axes, 0, 0, tiled=True)


def to_core(array):
    return lax.ppermute(array, "c", [(0, 1), (1, 0)])


def by_frames(array, by):
    pairs = [(i, i + by) for i in range(16) if 0 <= i + by < 16]
    return lax.ppermute(array, ("x", "z"), pairs)


def by_rows(array, by):
    pairs = [(i, i + by) for i in range(8) if 0 <= i + by < 8]
    return lax.ppermute(array, ("y", "c"), pairs)


def summed(own, send):
    got = to_core(send)
    (wide,) = on_chip(halves_body, [shape((16, 216, 128), BF16)], "halves")(own, got)
    (thin,) = on_chip(second_body, [shape((4, 216, 128), BF16)], "second")(
        exchanged(wide, ("x", "y"))
    )
    (wide,) = on_chip(third_body, [shape((16, 216, 128), BF16)], "third")(exchanged(thin, "z"))
    half = exchanged(wide, ("x", "y")).reshape(3456, 128)
    return half, to_core(half)


def on_device(clip_frames, enc_weight, dec_weight, out_grad):
    seg = lax.axis_index("segment")
    core = lax.axis_index("c")

    stage = pltpu.VMEM((136, 128), F32)
    (down,) = on_chip(edge_body, [shape((5, 128, 128), BF16)], "edge")(clip_frames, out_grad)
    above = by_rows(down, 1)
    below = by_rows(out_grad[:, 0:1], -1)
    (taps,) = on_chip(windows_body, [shape((4, 8, 64, 384), BF16)], "windows", scratch=[stage])(
        clip_frames
    )
    lat1, part, own0, tail, tops, cot = on_chip(
        encode_body,
        [
            shape((4, 64, 256), BF16),
            shape((4, 64, 256), PART),
            shape((4, 64, 256), F32),
            shape((2, 9, 128, 128), BF16),
            shape((4, 64, 384), BF16),
            shape((2, 6, 64, 128), BF16),
        ],
        "encode",
        scratch=[stage],
        grant=16,
    )(clip_frames, taps, above, enc_weight, out_grad, below)
    part = by_frames(part, 1)
    later_cot = by_frames(cot, -1)
    latent, down, up = on_chip(
        join_body,
        [
            shape((2, 4, 64, 256), BF16),
            shape((2, 2, 64, 256), BF16),
            shape((2, 2, 64, 256), BF16),
        ],
        "join",
    )(own0, part, lat1)
    top = by_rows(down, 1)
    bottom = by_rows(up, -1)
    tail, _ = lax.optimization_barrier((tail, down))
    tail = lax.ppermute(tail, ("segment", "x", "z"), [(16 + t - 1, t) for t in range(1, 16)])
    rows6 = (2, 6, 64, 128)
    own_part, behind, gone = on_chip(
        decode_body,
        [shape(rows6, F32), shape(rows6, PART), shape(rows6, PART)],
        "decode",
        scratch=[pltpu.VMEM((2, 8, 64, 768), BF16)],
        grant=14,
    )(latent, top, bottom, dec_weight)
    from_behind = by_frames(gone, 1)
    from_later = by_frames(behind, -1)
    seg = seg.reshape(1)
    tail, lat, _ = lax.optimization_barrier((tail, latent, gone))
    (turned,) = on_chip(
        turned_body,
        [shape((15, 384, 256), BF16)],
        "turned",
        1,
        [
            pltpu.VMEM((2, 64, 384), BF16),
            pltpu.VMEM((2, 8, 64, 384), BF16),
            pltpu.VMEM((2, 8, 64, 768), BF16),
            stage,
        ],
        16,
    )(seg, tail, tops, taps, lat, top, bottom)
    lat_grad, own, send = on_chip(
        grads_body,
        [
            shape((2, 4, 64, 256), BF16),
            shape((3456, 128), F32),
            shape((3456, 128), BF16),
        ],
        "grads",
        2,
        [
            pltpu.VMEM((6912, 128), F32),
            pltpu.VMEM((4, 6, 64, 128), BF16),
            pltpu.VMEM((4, 6, 64, 384), BF16),
        ],
        24,
    )(seg, core.reshape(1), own_part, from_behind, gone, from_later, cot, later_cot, dec_weight, turned)
    latent_pair = jnp.where(seg[0] == 0, lat_grad, latent)[None]
    half, other = summed(own, send)
    whole = jnp.where(core == 0, jnp.stack([half, other]), jnp.stack([other, half]))
    weight_grads = whole.reshape(27, 32768).astype(F32) * (1.0 / math.sqrt(32 * 32 * 64))
    return latent_pair, weight_grads[None]


def solution(mesh):
    fine = Mesh(mesh.devices.reshape(2, 4, 4, 4, 2), ("segment", "x", "z", "y", "c"))
    cells = P(("x", "z"), ("y", "c"), None, None)
    return jax.shard_map(
        on_device,
        mesh=fine,
        in_specs=(cells, P(), P(), cells),
        out_specs=(P("segment", ("x", "z"), ("y", "c"), None, None), P("segment", None, None)),
        check_vma=False,
    )
```

```python
import math

import jax
import jax.numpy as jnp
from jax import lax
from jax.experimental import pallas as pl
from jax.experimental.pallas import tpu as pltpu
from jax.sharding import Mesh, PartitionSpec as P

F32 = jnp.float32
BF16 = jnp.bfloat16
PART = BF16
MIB = 1024 * 1024


def shape(dims, dtype):
    return jax.ShapeDtypeStruct(dims, dtype)


def on_chip(body, outs, smem=0, scratch=(), grant=8, far=False):
    def call(*args):
        specs = [pl.BlockSpec(memory_space=pltpu.SMEM)] * smem
        specs += [pl.BlockSpec(memory_space=pl.ANY if far else pltpu.VMEM)] * (len(args) - smem)
        return pl.pallas_call(
            body,
            out_shape=outs,
            in_specs=specs,
            out_specs=[pl.BlockSpec(memory_space=pl.ANY if far else pltpu.VMEM)] * len(outs),
            scratch_shapes=list(scratch),
            compiler_params=pltpu.CompilerParams(vmem_limit_bytes=grant * MIB),
        )(*args)

    return call


def dot(left, right):
    return jnp.dot(left, right, preferred_element_type=F32)


def dot_nt(left, right):
    return lax.dot_general(left, right, (((1,), (1,)), ((), ())), preferred_element_type=F32)


def clip_windows(row, stage):
    stage[8:136, :] = row.astype(F32)
    before = stage[pl.ds(7, 64, stride=2), :]
    here = stage[pl.ds(8, 64, stride=2), :]
    after = stage[pl.ds(9, 64, stride=2), :]
    return jnp.concatenate([before, here, after], axis=1).astype(BF16)


def neighbour_cols(row):
    wide = row.astype(F32)
    place = lax.broadcasted_iota(jnp.int32, wide.shape, 0)
    last = wide.shape[0] - 1
    before = jnp.where(place == 0, 0.0, pltpu.roll(wide, 1, 0)).astype(BF16)
    after = jnp.where(place == last, 0.0, pltpu.roll(wide, last, 0)).astype(BF16)
    return before, row, after


def start_stage(stage):
    stage[0:8, :] = jnp.zeros((8, stage.shape[1]), F32)


def edge_body(seg_at, core_at, clip, cot, down, up, corner, tail, arrived):
    copies = [
        pltpu.make_async_copy(source, target, arrived.at[i])
        for i, (source, target) in enumerate(
            (
                (clip.at[:, 7], down.at[0:4]),
                (cot.at[0, 3], down.at[4, 0:64]),
                (cot.at[1, 3], down.at[4, 64:128]),
                (cot.at[:, 0], up),
                (clip.at[2:4, 7], corner),
                (clip.at[2:4], tail),
            )
        )
    ]
    for one in copies:
        one.start()
    for one in copies:
        one.wait()


def windows_body(clip, taps, stage):
    start_stage(stage)
    for f in range(4):

        def one(r, carry, f=f):
            taps[f, r] = clip_windows(clip[f, r], stage)
            return carry

        lax.fori_loop(0, 8, one, 0)


def clip_im2col(tops, taps, f, b):
    rows = [2 * h + b for h in range(4)]
    return jnp.concatenate([tops[f] if p == 0 else taps[f, p - 1] for p in rows], axis=0)


def encode_body(
    taps, above, weight, cot, below, lat1, part, own0, tops, rows6, stage
):
    start_stage(stage)
    for f in range(4):
        tops[f] = clip_windows(above[f], stage)

    def conv(f, a):
        total = None
        for b in range(3):
            term = dot(clip_im2col(tops, taps, f, b), weight[a, b].reshape(384, 256))
            total = term if total is None else total + term
        return total

    part[...] = (conv(2, 0) + conv(3, 1)).astype(part.dtype).reshape(4, 64, 256)
    lat1[...] = (conv(0, 0) + conv(1, 1) + conv(2, 2)).astype(BF16).reshape(4, 64, 256)
    own0[...] = conv(0, 2).reshape(4, 64, 256)
    rows6[0, 0] = above[4, 0:64]
    rows6[1, 0] = above[4, 64:128]
    rows6[:, 1:5] = cot[...]
    rows6[:, 5] = below[...]


def join_body(own0, part, lat1, lat, down, up):
    lat[0] = (own0[...] + part[...].astype(F32)).astype(BF16)
    lat[1] = lat1[...]
    down[...] = lat[:, 2:4]
    up[...] = lat[:, 0:2]


def fill_latent(lat, top, bottom, wide):
    for f in range(2):
        for r in range(2):
            wide[f, r] = jnp.concatenate(neighbour_cols(top[f, r]), axis=1)
            wide[f, 6 + r] = jnp.concatenate(neighbour_cols(bottom[f, r]), axis=1)

        def one(r, carry, f=f):
            wide[f, r + 2] = jnp.concatenate(neighbour_cols(lat[f, r]), axis=1)
            return carry

        lax.fori_loop(0, 4, one, 0)


def decode_body(lat, top, bottom, weight, own, behind, part, wide):
    fill_latent(lat, top, bottom, wide)

    def conv(f, a):
        total = None
        for b in range(3):
            window = wide[f, b : b + 6].reshape(384, 768)
            term = dot(window, weight[a, b].reshape(768, 128))
            total = term if total is None else total + term
        return total

    part[0] = (conv(0, 0) + conv(1, 1)).astype(part.dtype).reshape(6, 64, 128)
    part[1] = conv(1, 0).astype(part.dtype).reshape(6, 64, 128)
    own[0] = conv(0, 2).reshape(6, 64, 128)
    own[1] = (conv(0, 1) + conv(1, 2)).reshape(6, 64, 128)
    behind[...] = own[...].astype(behind.dtype)


def turned_body(seg_at, tail, corner, tops, taps, lat, top, bottom, turned, btops, btaps, wide, stage):
    seg = seg_at[0]

    @pl.when(seg == 0)
    def _():
        start_stage(stage)
        for f in range(2):
            btops[f] = clip_windows(corner[f], stage)

            def one(r, carry, f=f):
                btaps[f, r] = clip_windows(tail[f, r], stage)
                return carry

            lax.fori_loop(0, 8, one, 0)
        for f in range(5):
            for b in range(3):
                rows = clip_im2col(btops, btaps, f, b) if f < 2 else clip_im2col(tops, taps, f - 2, b)
                turned[f * 3 + b] = rows.T

    @pl.when(seg != 0)
    def _():
        fill_latent(lat, top, bottom, wide)
        for f in range(2):
            for b in range(3):
                flat = wide[f, b + 1 : b + 5].reshape(256, 768).T
                turned[(f * 3 + b) * 2] = flat[0:384]
                turned[(f * 3 + b) * 2 + 1] = flat[384:768]


def grads_body(
    seg_at, core_at, own_part, from_behind, gone, from_later, cot, later_cot, weight, turned,
    lat_grad, own, send, gathered, slopes, rim,
):
    seg = seg_at[0]
    core = core_at[0]

    def slope_of(pre, grad):
        sigm = jax.nn.sigmoid(pre)
        return (grad.astype(F32) * sigm * (1.0 + pre * (1.0 - sigm))).astype(BF16)

    slopes[0:2] = slope_of(own_part[...] + from_behind[...].astype(F32), cot[...])
    slopes[2:4] = slope_of(from_later[...].astype(F32) + gone[...].astype(F32), later_cot[...])

    @pl.when(seg == 0)
    def _():
        for f in range(4):
            for r in range(6):
                left, same, right = neighbour_cols(slopes[f, r])
                rim[f, r] = jnp.concatenate([right, same, left], axis=1)
        grads = []
        for t in range(2):
            total = None
            for a in range(3):
                for b in range(3):
                    window = rim[t + 2 - a, 2 - b : 6 - b].reshape(256, 384)
                    side = jnp.concatenate([weight[a, b, c] for c in range(3)], axis=1)
                    term = dot_nt(window, side)
                    total = term if total is None else total + term
            grad = total.astype(BF16)
            lat_grad[t] = grad.reshape(4, 64, 256)
            grads.append(grad)
        for a in range(3):
            for b in range(3):
                total = dot(turned[a * 3 + b], grads[0]) + dot(turned[(a + 2) * 3 + b], grads[1])
                for c in range(3):
                    tap = (a * 3 + b) * 3 + c
                    for j in range(2):
                        gathered[pl.ds(tap * 256 + j, 128, stride=2), :] = total[
                            c * 128 : (c + 1) * 128, j * 128 : (j + 1) * 128
                        ]

    @pl.when(seg != 0)
    def _():
        lat_grad[...] = jnp.zeros(lat_grad.shape, BF16)
        for a in range(3):
            for b in range(3):
                for i in range(2):
                    total = None
                    for f in range(2):
                        cells = slopes[f + 2 - a, 1:5].reshape(256, 128)
                        term = dot(turned[(f * 3 + b) * 2 + i], cells)
                        total = term if total is None else total + term
                    start = (a * 3 + b) * 768 + i * 384
                    gathered[start : start + 384, :] = total

    half = own.shape[0]
    own[...] = gathered[pl.ds(pl.multiple_of(core * half, 8), half), :]
    send[...] = gathered[pl.ds(pl.multiple_of((1 - core) * half, 8), half), :].astype(BF16)


def halves_body(own, got, spread):
    for j in range(16):
        rows = slice(216 * j, 216 * (j + 1))
        spread[j] = (own[rows, :] + got[rows, :].astype(F32)).astype(BF16)


def second_body(got, spread):
    total = got[0].astype(F32)
    for j in range(1, 16):
        total = total + got[j].astype(F32)
    for j in range(4):
        spread[j] = total.astype(BF16)


def third_body(got, spread):
    total = got[0].astype(F32)
    for j in range(1, 4):
        total = total + got[j].astype(F32)
    for j in range(16):
        spread[j] = total.astype(BF16)


def exchanged(array, axes):
    return lax.all_to_all(array, axes, 0, 0, tiled=True)


def to_core(array):
    return lax.ppermute(array, "c", [(0, 1), (1, 0)])


def by_frames(array, by):
    pairs = [(i, i + by) for i in range(16) if 0 <= i + by < 16]
    return lax.ppermute(array, ("x", "z"), pairs)


def by_rows(array, by):
    pairs = [(i, i + by) for i in range(8) if 0 <= i + by < 8]
    return lax.ppermute(array, ("y", "c"), pairs)


def summed(own, send):
    got = to_core(send)
    (wide,) = on_chip(halves_body, [shape((16, 216, 128), BF16)])(own, got)
    (thin,) = on_chip(second_body, [shape((4, 216, 128), BF16)])(exchanged(wide, ("x", "y")))
    (wide,) = on_chip(third_body, [shape((16, 216, 128), BF16)])(exchanged(thin, "z"))
    half = exchanged(wide, ("x", "y")).reshape(3456, 128)
    return half, to_core(half)


def on_device(clip_frames, enc_weight, dec_weight, out_grad):
    seg = lax.axis_index("segment")
    core = lax.axis_index("c")

    stage = pltpu.VMEM((136, 128), F32)
    seg = seg.reshape(1)
    core_at = core.reshape(1)
    down, up, corner, tail = on_chip(
        edge_body,
        [
            shape((5, 128, 128), BF16),
            shape((2, 64, 128), BF16),
            shape((2, 128, 128), BF16),
            shape((2, 8, 128, 128), BF16),
        ],
        2,
        [pltpu.SemaphoreType.DMA((6,))],
        60,
        True,
    )(seg, core_at, clip_frames, out_grad)
    above = by_rows(down, 1)
    below = by_rows(up, -1)
    pairs = [(16 + t - 1, t) for t in range(1, 16)]
    tail = lax.ppermute(tail, ("segment", "x", "z"), pairs)
    pairs = [(t * 8 + r, t * 8 + 8 + r + 1) for t in range(15) for r in range(7)]
    corner = lax.ppermute(corner, ("x", "z", "y", "c"), pairs)
    (taps,) = on_chip(windows_body, [shape((4, 8, 64, 384), BF16)], scratch=[stage])(clip_frames)
    lat1, part, own0, tops, cot = on_chip(
        encode_body,
        [
            shape((4, 64, 256), BF16),
            shape((4, 64, 256), PART),
            shape((4, 64, 256), F32),
            shape((4, 64, 384), BF16),
            shape((2, 6, 64, 128), BF16),
        ],
        scratch=[stage],
        grant=16,
    )(taps, above, enc_weight, out_grad, below)
    part = by_frames(part, 1)
    later_cot = by_frames(cot, -1)
    latent, down, up = on_chip(
        join_body,
        [
            shape((2, 4, 64, 256), BF16),
            shape((2, 2, 64, 256), BF16),
            shape((2, 2, 64, 256), BF16),
        ],
    )(own0, part, lat1)
    top = by_rows(down, 1)
    bottom = by_rows(up, -1)
    rows6 = (2, 6, 64, 128)
    own_part, behind, gone = on_chip(
        decode_body,
        [shape(rows6, F32), shape(rows6, PART), shape(rows6, PART)],
        scratch=[pltpu.VMEM((2, 8, 64, 768), BF16)],
        grant=14,
    )(latent, top, bottom, dec_weight)
    from_behind = by_frames(gone, 1)
    from_later = by_frames(behind, -1)
    tail, lat, _ = lax.optimization_barrier((tail, latent, gone))
    (turned,) = on_chip(
        turned_body,
        [shape((15, 384, 256), BF16)],
        1,
        [
            pltpu.VMEM((2, 64, 384), BF16),
            pltpu.VMEM((2, 8, 64, 384), BF16),
            pltpu.VMEM((2, 8, 64, 768), BF16),
            stage,
        ],
        16,
    )(seg, tail, corner, tops, taps, lat, top, bottom)
    lat_grad, own, send = on_chip(
        grads_body,
        [
            shape((2, 4, 64, 256), BF16),
            shape((3456, 128), F32),
            shape((3456, 128), BF16),
        ],
        2,
        [
            pltpu.VMEM((6912, 128), F32),
            pltpu.VMEM((4, 6, 64, 128), BF16),
            pltpu.VMEM((4, 6, 64, 384), BF16),
        ],
        24,
    )(seg, core_at, own_part, from_behind, gone, from_later, cot, later_cot, dec_weight, turned)
    latent_pair = jnp.where(seg[0] == 0, lat_grad, latent)[None]
    half, other = summed(own, send)
    whole = jnp.where(core == 0, jnp.stack([half, other]), jnp.stack([other, half]))
    weight_grads = whole.reshape(27, 32768).astype(F32) * (1.0 / math.sqrt(32 * 32 * 64))
    return latent_pair, weight_grads[None]


def solution(mesh):
    fine = Mesh(mesh.devices.reshape(2, 4, 4, 4, 2), ("segment", "x", "z", "y", "c"))
    cells = P(("x", "z"), ("y", "c"), None, None)

    return jax.shard_map(
        on_device,
        mesh=fine,
        in_specs=(cells, P(), P(), cells),
        out_specs=(P("segment", ("x", "z"), ("y", "c"), None, None), P("segment", None, None)),
        check_vma=False,
    )
```

```python
import math

import jax
import jax.numpy as jnp
from jax import lax
from jax.experimental import pallas as pl
from jax.experimental.pallas import tpu as pltpu
from jax.sharding import Mesh, PartitionSpec as P

F32 = jnp.float32
BF16 = jnp.bfloat16
PART = BF16
MIB = 1024 * 1024


def shape(dims, dtype):
    return jax.ShapeDtypeStruct(dims, dtype)


def on_chip(body, outs, smem=0, scratch=(), grant=8, far=False):
    def call(*args):
        specs = [pl.BlockSpec(memory_space=pltpu.SMEM)] * smem
        specs += [pl.BlockSpec(memory_space=pl.ANY if far else pltpu.VMEM)] * (len(args) - smem)
        return pl.pallas_call(
            body,
            out_shape=outs,
            in_specs=specs,
            out_specs=[pl.BlockSpec(memory_space=pltpu.VMEM)] * len(outs),
            scratch_shapes=list(scratch),
            compiler_params=pltpu.CompilerParams(vmem_limit_bytes=grant * MIB),
        )(*args)

    return call


def dot(left, right):
    return jnp.dot(left, right, preferred_element_type=F32)


def dot_nt(left, right):
    return lax.dot_general(left, right, (((1,), (1,)), ((), ())), preferred_element_type=F32)


def clip_windows(row, stage):
    stage[8:136, :] = row.astype(F32)
    before = stage[pl.ds(7, 64, stride=2), :]
    here = stage[pl.ds(8, 64, stride=2), :]
    after = stage[pl.ds(9, 64, stride=2), :]
    return jnp.concatenate([before, here, after], axis=1).astype(BF16)


def neighbour_cols(row):
    wide = row.astype(F32)
    place = lax.broadcasted_iota(jnp.int32, wide.shape, 0)
    last = wide.shape[0] - 1
    before = jnp.where(place == 0, 0.0, pltpu.roll(wide, 1, 0)).astype(BF16)
    after = jnp.where(place == last, 0.0, pltpu.roll(wide, last, 0)).astype(BF16)
    return before, row, after


def start_stage(stage):
    stage[0:8, :] = jnp.zeros((8, stage.shape[1]), F32)


def edge_body(seg_at, core_at, clip, cot, down, up, tail, arrived):
    copies = [
        pltpu.make_async_copy(source, target, arrived.at[i])
        for i, (source, target) in enumerate(
            (
                (clip.at[:, 7], down.at[0:4]),
                (cot.at[0, 3], down.at[4, 0:64]),
                (cot.at[1, 3], down.at[4, 64:128]),
                (cot.at[:, 0], up),
                (clip.at[2:4], tail),
            )
        )
    ]
    for one in copies:
        one.start()
    for one in copies:
        one.wait()


def windows_body(clip, taps, stage):
    start_stage(stage)
    for f in range(4):

        def one(r, carry, f=f):
            taps[f, r] = clip_windows(clip[f, r], stage)
            return carry

        lax.fori_loop(0, 8, one, 0)


def clip_im2col(tops, taps, f, b):
    rows = [2 * h + b for h in range(4)]
    return jnp.concatenate([tops[f] if p == 0 else taps[f, p - 1] for p in rows], axis=0)


def encode_body(
    taps, above, weight, cot, below, lat1, part, own0, tops, rows6, stage
):
    start_stage(stage)
    for f in range(4):
        tops[f] = clip_windows(above[f], stage)

    def conv(f, a):
        total = None
        for b in range(3):
            term = dot(clip_im2col(tops, taps, f, b), weight[a, b].reshape(384, 256))
            total = term if total is None else total + term
        return total

    part[...] = (conv(2, 0) + conv(3, 1)).astype(part.dtype).reshape(4, 64, 256)
    lat1[...] = (conv(0, 0) + conv(1, 1) + conv(2, 2)).astype(BF16).reshape(4, 64, 256)
    own0[...] = conv(0, 2).reshape(4, 64, 256)
    rows6[0, 0] = above[4, 0:64]
    rows6[1, 0] = above[4, 64:128]
    rows6[:, 1:5] = cot[...]
    rows6[:, 5] = below[...]


def join_body(own0, part, lat1, tail, lat, down, up):
    lat[0] = (own0[...] + part[...].astype(F32)).astype(BF16)
    lat[1] = lat1[...]
    down[:, 0:2] = lat[:, 2:4]
    down[:, 2, :, 0:128] = tail[:, 7, 0:64]
    down[:, 2, :, 128:256] = tail[:, 7, 64:128]
    up[...] = lat[:, 0:2]


def fill_latent(lat, top, bottom, wide):
    for f in range(2):
        for r in range(2):
            wide[f, r] = jnp.concatenate(neighbour_cols(top[f, r]), axis=1)
            wide[f, 6 + r] = jnp.concatenate(neighbour_cols(bottom[f, r]), axis=1)

        def one(r, carry, f=f):
            wide[f, r + 2] = jnp.concatenate(neighbour_cols(lat[f, r]), axis=1)
            return carry

        lax.fori_loop(0, 4, one, 0)


def decode_body(lat, top, bottom, weight, own, behind, part, wide):
    fill_latent(lat, top, bottom, wide)

    def conv(f, a):
        total = None
        for b in range(3):
            window = wide[f, b : b + 6].reshape(384, 768)
            term = dot(window, weight[a, b].reshape(768, 128))
            total = term if total is None else total + term
        return total

    part[0] = (conv(0, 0) + conv(1, 1)).astype(part.dtype).reshape(6, 64, 128)
    part[1] = conv(1, 0).astype(part.dtype).reshape(6, 64, 128)
    own[0] = conv(0, 2).reshape(6, 64, 128)
    own[1] = (conv(0, 1) + conv(1, 2)).reshape(6, 64, 128)
    behind[...] = own[...].astype(behind.dtype)


def turned_body(seg_at, tail, tops, taps, lat, top, bottom, turned, btops, btaps, wide, stage):
    seg = seg_at[0]

    @pl.when(seg == 0)
    def _():
        start_stage(stage)
        for f in range(2):
            corner = jnp.concatenate([top[f, 2, :, 0:128], top[f, 2, :, 128:256]], axis=0)
            btops[f] = clip_windows(corner, stage)

            def one(r, carry, f=f):
                btaps[f, r] = clip_windows(tail[f, r], stage)
                return carry

            lax.fori_loop(0, 8, one, 0)
        for f in range(5):
            for b in range(3):
                rows = clip_im2col(btops, btaps, f, b) if f < 2 else clip_im2col(tops, taps, f - 2, b)
                turned[f * 3 + b] = rows.T

    @pl.when(seg != 0)
    def _():
        fill_latent(lat, top, bottom, wide)
        for f in range(2):
            for b in range(3):
                flat = wide[f, b + 1 : b + 5].reshape(256, 768).T
                turned[(f * 3 + b) * 2] = flat[0:384]
                turned[(f * 3 + b) * 2 + 1] = flat[384:768]


def grads_body(
    seg_at, core_at, own_part, from_behind, gone, from_later, cot, later_cot, weight, turned,
    lat_grad, own, send, gathered, slopes, rim,
):
    seg = seg_at[0]
    core = core_at[0]

    def slope_of(pre, grad):
        sigm = jax.nn.sigmoid(pre)
        return (grad.astype(F32) * sigm * (1.0 + pre * (1.0 - sigm))).astype(BF16)

    slopes[0:2] = slope_of(own_part[...] + from_behind[...].astype(F32), cot[...])
    slopes[2:4] = slope_of(from_later[...].astype(F32) + gone[...].astype(F32), later_cot[...])

    @pl.when(seg == 0)
    def _():
        for f in range(4):
            for r in range(6):
                left, same, right = neighbour_cols(slopes[f, r])
                rim[f, r] = jnp.concatenate([right, same, left], axis=1)
        grads = []
        for t in range(2):
            total = None
            for a in range(3):
                for b in range(3):
                    window = rim[t + 2 - a, 2 - b : 6 - b].reshape(256, 384)
                    side = jnp.concatenate([weight[a, b, c] for c in range(3)], axis=1)
                    term = dot_nt(window, side)
                    total = term if total is None else total + term
            grad = total.astype(BF16)
            lat_grad[t] = grad.reshape(4, 64, 256)
            grads.append(grad)
        for a in range(3):
            for b in range(3):
                total = dot(turned[a * 3 + b], grads[0]) + dot(turned[(a + 2) * 3 + b], grads[1])
                for c in range(3):
                    tap = (a * 3 + b) * 3 + c
                    for j in range(2):
                        gathered[pl.ds(tap * 256 + j, 128, stride=2), :] = total[
                            c * 128 : (c + 1) * 128, j * 128 : (j + 1) * 128
                        ]

    @pl.when(seg != 0)
    def _():
        lat_grad[...] = jnp.zeros(lat_grad.shape, BF16)
        for a in range(3):
            for b in range(3):
                for i in range(2):
                    total = None
                    for f in range(2):
                        cells = slopes[f + 2 - a, 1:5].reshape(256, 128)
                        term = dot(turned[(f * 3 + b) * 2 + i], cells)
                        total = term if total is None else total + term
                    start = (a * 3 + b) * 768 + i * 384
                    gathered[start : start + 384, :] = total

    half = own.shape[0]
    own[...] = gathered[pl.ds(pl.multiple_of(core * half, 8), half), :]
    send[...] = gathered[pl.ds(pl.multiple_of((1 - core) * half, 8), half), :].astype(BF16)


def halves_body(own, got, spread):
    for j in range(16):
        rows = slice(216 * j, 216 * (j + 1))
        spread[j] = (own[rows, :] + got[rows, :].astype(F32)).astype(BF16)


def second_body(got, spread):
    total = got[0].astype(F32)
    for j in range(1, 16):
        total = total + got[j].astype(F32)
    for j in range(4):
        spread[j] = total.astype(BF16)


def third_body(got, spread):
    total = got[0].astype(F32)
    for j in range(1, 4):
        total = total + got[j].astype(F32)
    for j in range(16):
        spread[j] = total.astype(BF16)


def exchanged(array, axes):
    return lax.all_to_all(array, axes, 0, 0, tiled=True)


def to_core(array):
    return lax.ppermute(array, "c", [(0, 1), (1, 0)])


def by_frames(array, by):
    pairs = [(i, i + by) for i in range(16) if 0 <= i + by < 16]
    return lax.ppermute(array, ("x", "z"), pairs)


def by_rows(array, by):
    pairs = [(i, i + by) for i in range(8) if 0 <= i + by < 8]
    return lax.ppermute(array, ("y", "c"), pairs)


def summed(own, send):
    got = to_core(send)
    (wide,) = on_chip(halves_body, [shape((16, 216, 128), BF16)])(own, got)
    (thin,) = on_chip(second_body, [shape((4, 216, 128), BF16)])(exchanged(wide, ("x", "y")))
    (wide,) = on_chip(third_body, [shape((16, 216, 128), BF16)])(exchanged(thin, "z"))
    half = exchanged(wide, ("x", "y")).reshape(3456, 128)
    return half, to_core(half)


def on_device(clip_frames, enc_weight, dec_weight, out_grad):
    seg = lax.axis_index("segment")
    core = lax.axis_index("c")

    stage = pltpu.VMEM((136, 128), F32)
    seg = seg.reshape(1)
    core_at = core.reshape(1)
    down, up, tail = on_chip(
        edge_body,
        [
            shape((5, 128, 128), BF16),
            shape((2, 64, 128), BF16),
            shape((2, 8, 128, 128), BF16),
        ],
        2,
        [pltpu.SemaphoreType.DMA((5,))],
        60,
        True,
    )(seg, core_at, clip_frames, out_grad)
    above = by_rows(down, 1)
    below = by_rows(up, -1)
    pairs = [(16 + t - 1, t) for t in range(1, 16)]
    tail = lax.ppermute(tail, ("segment", "x", "z"), pairs)
    (taps,) = on_chip(windows_body, [shape((4, 8, 64, 384), BF16)], scratch=[stage])(clip_frames)
    lat1, part, own0, tops, cot = on_chip(
        encode_body,
        [
            shape((4, 64, 256), BF16),
            shape((4, 64, 256), PART),
            shape((4, 64, 256), F32),
            shape((4, 64, 384), BF16),
            shape((2, 6, 64, 128), BF16),
        ],
        scratch=[stage],
        grant=16,
    )(taps, above, enc_weight, out_grad, below)
    part = by_frames(part, 1)
    later_cot = by_frames(cot, -1)
    latent, down, up = on_chip(
        join_body,
        [
            shape((2, 4, 64, 256), BF16),
            shape((2, 3, 64, 256), BF16),
            shape((2, 2, 64, 256), BF16),
        ],
    )(own0, part, lat1, tail)
    top = by_rows(down, 1)
    bottom = by_rows(up, -1)
    rows6 = (2, 6, 64, 128)
    own_part, behind, gone = on_chip(
        decode_body,
        [shape(rows6, F32), shape(rows6, PART), shape(rows6, PART)],
        scratch=[pltpu.VMEM((2, 8, 64, 768), BF16)],
        grant=14,
    )(latent, top, bottom, dec_weight)
    from_behind = by_frames(gone, 1)
    from_later = by_frames(behind, -1)
    tail, lat, _ = lax.optimization_barrier((tail, latent, gone))
    (turned,) = on_chip(
        turned_body,
        [shape((15, 384, 256), BF16)],
        1,
        [
            pltpu.VMEM((2, 64, 384), BF16),
            pltpu.VMEM((2, 8, 64, 384), BF16),
            pltpu.VMEM((2, 8, 64, 768), BF16),
            stage,
        ],
        16,
    )(seg, tail, tops, taps, lat, top, bottom)
    lat_grad, own, send = on_chip(
        grads_body,
        [
            shape((2, 4, 64, 256), BF16),
            shape((3456, 128), F32),
            shape((3456, 128), BF16),
        ],
        2,
        [
            pltpu.VMEM((6912, 128), F32),
            pltpu.VMEM((4, 6, 64, 128), BF16),
            pltpu.VMEM((4, 6, 64, 384), BF16),
        ],
        24,
    )(seg, core_at, own_part, from_behind, gone, from_later, cot, later_cot, dec_weight, turned)
    latent_pair = jnp.where(seg[0] == 0, lat_grad, latent)[None]
    half, other = summed(own, send)
    whole = jnp.where(core == 0, jnp.stack([half, other]), jnp.stack([other, half]))
    weight_grads = whole.reshape(27, 32768).astype(F32) * (1.0 / math.sqrt(32 * 32 * 64))
    return latent_pair, weight_grads[None]


def solution(mesh):
    fine = Mesh(mesh.devices.reshape(2, 4, 4, 4, 2), ("segment", "x", "z", "y", "c"))
    cells = P(("x", "z"), ("y", "c"), None, None)

    return jax.shard_map(
        on_device,
        mesh=fine,
        in_specs=(cells, P(), P(), cells),
        out_specs=(P("segment", ("x", "z"), ("y", "c"), None, None), P("segment", None, None)),
        check_vma=False,
    )
```

```python
import math

import jax
import jax.numpy as jnp
from jax import lax
from jax.experimental import pallas as pl
from jax.experimental.pallas import tpu as pltpu
from jax.sharding import Mesh, PartitionSpec as P

F32 = jnp.float32
BF16 = jnp.bfloat16
PART = BF16
MIB = 1024 * 1024


def shape(dims, dtype):
    return jax.ShapeDtypeStruct(dims, dtype)


def on_chip(body, outs, smem=0, scratch=(), grant=8):
    def call(*args):
        specs = [pl.BlockSpec(memory_space=pltpu.SMEM)] * smem
        specs += [pl.BlockSpec(memory_space=pltpu.VMEM)] * (len(args) - smem)
        return pl.pallas_call(
            body,
            out_shape=outs,
            in_specs=specs,
            out_specs=[pl.BlockSpec(memory_space=pltpu.VMEM)] * len(outs),
            scratch_shapes=list(scratch),
            compiler_params=pltpu.CompilerParams(vmem_limit_bytes=grant * MIB),
        )(*args)

    return call


def dot(left, right):
    return jnp.dot(left, right, preferred_element_type=F32)


def dot_nt(left, right):
    return lax.dot_general(left, right, (((1,), (1,)), ((), ())), preferred_element_type=F32)


def clip_windows(row, stage):
    stage[8:136, :] = row.astype(F32)
    before = stage[pl.ds(7, 64, stride=2), :]
    here = stage[pl.ds(8, 64, stride=2), :]
    after = stage[pl.ds(9, 64, stride=2), :]
    return jnp.concatenate([before, here, after], axis=1).astype(BF16)


def neighbour_cols(row):
    wide = row.astype(F32)
    place = lax.broadcasted_iota(jnp.int32, wide.shape, 0)
    last = wide.shape[0] - 1
    before = jnp.where(place == 0, 0.0, pltpu.roll(wide, 1, 0)).astype(BF16)
    after = jnp.where(place == last, 0.0, pltpu.roll(wide, last, 0)).astype(BF16)
    return before, row, after


def start_stage(stage):
    stage[0:8, :] = jnp.zeros((8, stage.shape[1]), F32)


def edge_body(seg_at, core_at, clip, down, tail):
    down[...] = clip[:, 7]
    tail[...] = clip[2:4]


def windows_body(clip, taps, stage):
    start_stage(stage)
    for f in range(4):

        def one(r, carry, f=f):
            taps[f, r] = clip_windows(clip[f, r], stage)
            return carry

        lax.fori_loop(0, 8, one, 0)


def clip_im2col(tops, taps, f, b):
    rows = [2 * h + b for h in range(4)]
    return jnp.concatenate([tops[f] if p == 0 else taps[f, p - 1] for p in rows], axis=0)


def encode_body(
    taps, above, weight, lat1, part, own0, tops, stage
):
    start_stage(stage)
    for f in range(4):
        tops[f] = clip_windows(above[f], stage)

    def conv(f, a):
        total = None
        for b in range(3):
            term = dot(clip_im2col(tops, taps, f, b), weight[a, b].reshape(384, 256))
            total = term if total is None else total + term
        return total

    part[...] = (conv(2, 0) + conv(3, 1)).astype(part.dtype).reshape(4, 64, 256)
    lat1[...] = (conv(0, 0) + conv(1, 1) + conv(2, 2)).astype(BF16).reshape(4, 64, 256)
    own0[...] = conv(0, 2).reshape(4, 64, 256)


def join_body(own0, part, lat1, tail, cot, later_cot, lat, down, up):
    lat[0] = (own0[...] + part[...].astype(F32)).astype(BF16)
    lat[1] = lat1[...]
    down[:, 0:2] = lat[:, 2:4]
    down[:, 2, :, 0:128] = tail[:, 7, 0:64]
    down[:, 2, :, 128:256] = tail[:, 7, 64:128]
    down[:, 3, :, 0:128] = cot[:, 3]
    down[:, 3, :, 128:256] = later_cot[:, 3]
    up[:, 0:2] = lat[:, 0:2]
    up[:, 2, :, 0:128] = cot[:, 0]
    up[:, 2, :, 128:256] = later_cot[:, 0]


def fill_latent(lat, top, bottom, wide):
    for f in range(2):
        for r in range(2):
            wide[f, r] = jnp.concatenate(neighbour_cols(top[f, r]), axis=1)
            wide[f, 6 + r] = jnp.concatenate(neighbour_cols(bottom[f, r]), axis=1)

        def one(r, carry, f=f):
            wide[f, r + 2] = jnp.concatenate(neighbour_cols(lat[f, r]), axis=1)
            return carry

        lax.fori_loop(0, 4, one, 0)


def decode_body(lat, top, bottom, weight, own, behind, part, wide):
    fill_latent(lat, top, bottom, wide)

    def conv(f, a):
        total = None
        for b in range(3):
            window = wide[f, b : b + 6].reshape(384, 768)
            term = dot(window, weight[a, b].reshape(768, 128))
            total = term if total is None else total + term
        return total

    part[0] = (conv(0, 0) + conv(1, 1)).astype(part.dtype).reshape(6, 64, 128)
    part[1] = conv(1, 0).astype(part.dtype).reshape(6, 64, 128)
    own[0] = conv(0, 2).reshape(6, 64, 128)
    own[1] = (conv(0, 1) + conv(1, 2)).reshape(6, 64, 128)
    behind[...] = own[...].astype(behind.dtype)


def turned_body(seg_at, tail, tops, taps, lat, top, bottom, turned, btops, btaps, wide, stage):
    seg = seg_at[0]

    @pl.when(seg == 0)
    def _():
        start_stage(stage)
        for f in range(2):
            corner = jnp.concatenate([top[f, 2, :, 0:128], top[f, 2, :, 128:256]], axis=0)
            btops[f] = clip_windows(corner, stage)

            def one(r, carry, f=f):
                btaps[f, r] = clip_windows(tail[f, r], stage)
                return carry

            lax.fori_loop(0, 8, one, 0)
        for f in range(5):
            for b in range(3):
                rows = clip_im2col(btops, btaps, f, b) if f < 2 else clip_im2col(tops, taps, f - 2, b)
                turned[f * 3 + b] = rows.T

    @pl.when(seg != 0)
    def _():
        fill_latent(lat, top, bottom, wide)
        for f in range(2):
            for b in range(3):
                flat = wide[f, b + 1 : b + 5].reshape(256, 768).T
                turned[(f * 3 + b) * 2] = flat[0:384]
                turned[(f * 3 + b) * 2 + 1] = flat[384:768]


def grads_body(
    seg_at, core_at, own_part, from_behind, gone, from_later, cot, later_cot, top, bottom,
    weight, turned,
    lat_grad, own, send, gathered, slopes, rim,
):
    seg = seg_at[0]
    core = core_at[0]

    def slope_at(start, rows, pre, grad):
        sigm = jax.nn.sigmoid(pre[:, rows])
        scaled = grad.astype(F32) * sigm * (1.0 + pre[:, rows] * (1.0 - sigm))
        slopes[start : start + 2, rows] = scaled.astype(BF16)

    for start, one, other, mid, lanes in (
        (0, own_part, from_behind, cot, slice(0, 128)),
        (2, from_later, gone, later_cot, slice(128, 256)),
    ):
        pre = one[...].astype(F32) + other[...].astype(F32)
        slope_at(start, slice(0, 1), pre, top[:, 3:4, :, lanes])
        slope_at(start, slice(1, 5), pre, mid[...])
        slope_at(start, slice(5, 6), pre, bottom[:, 2:3, :, lanes])

    @pl.when(seg == 0)
    def _():
        for f in range(4):
            for r in range(6):
                left, same, right = neighbour_cols(slopes[f, r])
                rim[f, r] = jnp.concatenate([right, same, left], axis=1)
        grads = []
        for t in range(2):
            total = None
            for a in range(3):
                for b in range(3):
                    window = rim[t + 2 - a, 2 - b : 6 - b].reshape(256, 384)
                    side = jnp.concatenate([weight[a, b, c] for c in range(3)], axis=1)
                    term = dot_nt(window, side)
                    total = term if total is None else total + term
            grad = total.astype(BF16)
            lat_grad[t] = grad.reshape(4, 64, 256)
            grads.append(grad)
        for a in range(3):
            for b in range(3):
                total = dot(turned[a * 3 + b], grads[0]) + dot(turned[(a + 2) * 3 + b], grads[1])
                for c in range(3):
                    tap = (a * 3 + b) * 3 + c
                    for j in range(2):
                        gathered[pl.ds(tap * 256 + j, 128, stride=2), :] = total[
                            c * 128 : (c + 1) * 128, j * 128 : (j + 1) * 128
                        ]

    @pl.when(seg != 0)
    def _():
        lat_grad[...] = jnp.zeros(lat_grad.shape, BF16)
        for a in range(3):
            for b in range(3):
                for i in range(2):
                    total = None
                    for f in range(2):
                        cells = slopes[f + 2 - a, 1:5].reshape(256, 128)
                        term = dot(turned[(f * 3 + b) * 2 + i], cells)
                        total = term if total is None else total + term
                    start = (a * 3 + b) * 768 + i * 384
                    gathered[start : start + 384, :] = total

    half = own.shape[0]
    own[...] = gathered[pl.ds(pl.multiple_of(core * half, 8), half), :]
    send[...] = gathered[pl.ds(pl.multiple_of((1 - core) * half, 8), half), :].astype(BF16)


def halves_body(own, got, spread):
    for j in range(16):
        rows = slice(216 * j, 216 * (j + 1))
        spread[j] = (own[rows, :] + got[rows, :].astype(F32)).astype(BF16)


def second_body(got, spread):
    total = got[0].astype(F32)
    for j in range(1, 16):
        total = total + got[j].astype(F32)
    for j in range(4):
        spread[j] = total.astype(BF16)


def third_body(got, spread):
    total = got[0].astype(F32)
    for j in range(1, 4):
        total = total + got[j].astype(F32)
    for j in range(16):
        spread[j] = total.astype(BF16)


def exchanged(array, axes):
    return lax.all_to_all(array, axes, 0, 0, tiled=True)


def to_core(array):
    return lax.ppermute(array, "c", [(0, 1), (1, 0)])


def by_frames(array, by):
    pairs = [(i, i + by) for i in range(16) if 0 <= i + by < 16]
    return lax.ppermute(array, ("x", "z"), pairs)


def by_rows(array, by):
    pairs = [(i, i + by) for i in range(8) if 0 <= i + by < 8]
    return lax.ppermute(array, ("y", "c"), pairs)


def pair_body(seg_at, lat_grad, latent, pair):
    pair[...] = jnp.where(seg_at[0] == 0, lat_grad[...], latent[...])


def scaled_body(core_at, half, out):
    out[0] = half[...].astype(F32) * (1.0 / math.sqrt(32 * 32 * 64))


def half_written(core_at, half):
    return pl.pallas_call(
        scaled_body,
        out_shape=shape((2, 3456, 128), F32),
        grid_spec=pltpu.PrefetchScalarGridSpec(
            num_scalar_prefetch=1,
            grid=(4,),
            in_specs=[pl.BlockSpec((864, 128), lambda i, core: (i, 0))],
            out_specs=pl.BlockSpec((1, 864, 128), lambda i, core: (core[0], i, 0)),
        ),
        name="half_written",
        compiler_params=pltpu.CompilerParams(vmem_limit_bytes=8 * MIB),
    )(core_at, half)


def other_body(core_at, half, written, out):
    scaled_body(core_at, half, out)


def other_written(core_at, half, written):
    return pl.pallas_call(
        other_body,
        out_shape=shape((2, 3456, 128), F32),
        grid_spec=pltpu.PrefetchScalarGridSpec(
            num_scalar_prefetch=1,
            grid=(4,),
            in_specs=[
                pl.BlockSpec((864, 128), lambda i, core: (i, 0)),
                pl.BlockSpec(memory_space=pl.ANY),
            ],
            out_specs=pl.BlockSpec((1, 864, 128), lambda i, core: (1 - core[0], i, 0)),
        ),
        input_output_aliases={2: 0},
        name="other_written",
        compiler_params=pltpu.CompilerParams(vmem_limit_bytes=8 * MIB),
    )(core_at, half, written)


def summed(own, send):
    got = to_core(send)
    (wide,) = on_chip(halves_body, [shape((16, 216, 128), BF16)])(own, got)
    (thin,) = on_chip(second_body, [shape((4, 216, 128), BF16)])(exchanged(wide, ("x", "y")))
    (wide,) = on_chip(third_body, [shape((16, 216, 128), BF16)])(exchanged(thin, "z"))
    half = exchanged(wide, ("x", "y")).reshape(3456, 128)
    other = to_core(half)
    return half, other


def on_device(clip_frames, enc_weight, dec_weight, out_grad):
    seg = lax.axis_index("segment")
    core = lax.axis_index("c")

    stage = pltpu.VMEM((136, 128), F32)
    seg = seg.reshape(1)
    core_at = core.reshape(1)
    down, tail = on_chip(
        edge_body, [shape((4, 128, 128), BF16), shape((2, 8, 128, 128), BF16)], 2
    )(seg, core_at, clip_frames)
    above = by_rows(down, 1)
    pairs = [(16 + t - 1, t) for t in range(1, 16)]
    tail = lax.ppermute(tail, ("segment", "x", "z"), pairs)
    (taps,) = on_chip(windows_body, [shape((4, 8, 64, 384), BF16)], scratch=[stage])(clip_frames)
    lat1, part, own0, tops = on_chip(
        encode_body,
        [
            shape((4, 64, 256), BF16),
            shape((4, 64, 256), PART),
            shape((4, 64, 256), F32),
            shape((4, 64, 384), BF16),
        ],
        scratch=[stage],
        grant=16,
    )(taps, above, enc_weight)
    part = by_frames(part, 1)
    later_cot = by_frames(out_grad, -1)
    latent, down, up = on_chip(
        join_body,
        [
            shape((2, 4, 64, 256), BF16),
            shape((2, 4, 64, 256), BF16),
            shape((2, 3, 64, 256), BF16),
        ],
    )(own0, part, lat1, tail, out_grad, later_cot)
    top = by_rows(down, 1)
    bottom = by_rows(up, -1)
    rows6 = (2, 6, 64, 128)
    own_part, behind, gone = on_chip(
        decode_body,
        [shape(rows6, F32), shape(rows6, PART), shape(rows6, PART)],
        scratch=[pltpu.VMEM((2, 8, 64, 768), BF16)],
        grant=14,
    )(latent, top, bottom, dec_weight)
    from_behind = by_frames(gone, 1)
    from_later = by_frames(behind, -1)
    tail, lat, _ = lax.optimization_barrier((tail, latent, gone))
    (turned,) = on_chip(
        turned_body,
        [shape((15, 384, 256), BF16)],
        1,
        [
            pltpu.VMEM((2, 64, 384), BF16),
            pltpu.VMEM((2, 8, 64, 384), BF16),
            pltpu.VMEM((2, 8, 64, 768), BF16),
            stage,
        ],
        16,
    )(seg, tail, tops, taps, lat, top, bottom)
    lat_grad, own, send = on_chip(
        grads_body,
        [
            shape((2, 4, 64, 256), BF16),
            shape((3456, 128), F32),
            shape((3456, 128), BF16),
        ],
        2,
        [
            pltpu.VMEM((6912, 128), F32),
            pltpu.VMEM((4, 6, 64, 128), BF16),
            pltpu.VMEM((4, 6, 64, 384), BF16),
        ],
        24,
    )(seg, core_at, own_part, from_behind, gone, from_later, out_grad, later_cot, top, bottom, dec_weight, turned)
    (latent_pair,) = on_chip(pair_body, [shape((2, 4, 64, 256), BF16)], 1)(seg, lat_grad, latent)
    half, other = summed(own, send)
    grads = half_written(core_at, half)
    grads = other_written(core_at, other, grads)
    return latent_pair[None], grads.reshape(1, 27, 32768)


def solution(mesh):
    fine = Mesh(mesh.devices.reshape(2, 4, 4, 4, 2), ("segment", "x", "z", "y", "c"))
    cells = P(("x", "z"), ("y", "c"), None, None)

    return jax.shard_map(
        on_device,
        mesh=fine,
        in_specs=(cells, P(), P(), cells),
        out_specs=(P("segment", ("x", "z"), ("y", "c"), None, None), P("segment", None, None)),
        check_vma=False,
    )
```

```python
import math

import jax
import jax.numpy as jnp
from jax import lax
from jax.experimental import pallas as pl
from jax.experimental.pallas import tpu as pltpu
from jax.sharding import Mesh, PartitionSpec as P

F32 = jnp.float32
BF16 = jnp.bfloat16
PART = BF16
MIB = 1024 * 1024


def shape(dims, dtype):
    return jax.ShapeDtypeStruct(dims, dtype)


def on_chip(body, outs, smem=0, scratch=(), grant=8):
    def call(*args):
        specs = [pl.BlockSpec(memory_space=pltpu.SMEM)] * smem
        specs += [pl.BlockSpec(memory_space=pltpu.VMEM)] * (len(args) - smem)
        return pl.pallas_call(
            body,
            out_shape=outs,
            in_specs=specs,
            out_specs=[pl.BlockSpec(memory_space=pltpu.VMEM)] * len(outs),
            scratch_shapes=list(scratch),
            compiler_params=pltpu.CompilerParams(vmem_limit_bytes=grant * MIB),
        )(*args)

    return call


def dot(left, right):
    return jnp.dot(left, right, preferred_element_type=F32)


def dot_nt(left, right):
    return lax.dot_general(left, right, (((1,), (1,)), ((), ())), preferred_element_type=F32)


def clip_windows(row, stage):
    stage[8:136, :] = row.astype(F32)
    before = stage[pl.ds(7, 64, stride=2), :]
    here = stage[pl.ds(8, 64, stride=2), :]
    after = stage[pl.ds(9, 64, stride=2), :]
    return jnp.concatenate([before, here, after], axis=1).astype(BF16)


def neighbour_cols(row):
    wide = row.astype(F32)
    place = lax.broadcasted_iota(jnp.int32, wide.shape, 0)
    last = wide.shape[0] - 1
    before = jnp.where(place == 0, 0.0, pltpu.roll(wide, 1, 0)).astype(BF16)
    after = jnp.where(place == last, 0.0, pltpu.roll(wide, last, 0)).astype(BF16)
    return before, row, after


def start_stage(stage):
    stage[0:8, :] = jnp.zeros((8, stage.shape[1]), F32)


def edge_body(seg_at, core_at, clip, down):
    down[...] = clip[:, 7]


def windows_body(clip, taps, stage):
    start_stage(stage)
    for f in range(4):

        def one(r, carry, f=f):
            taps[f, r] = clip_windows(clip[f, r], stage)
            return carry

        lax.fori_loop(0, 8, one, 0)


def clip_im2col(tops, taps, f, b):
    rows = [2 * h + b for h in range(4)]
    return jnp.concatenate([tops[f] if p == 0 else taps[f, p - 1] for p in rows], axis=0)


def encode_body(
    clip, taps, above, weight, lat1, part, own0, tops, tail, stage
):
    start_stage(stage)
    for f in range(4):
        tops[f] = clip_windows(above[f], stage)

    def conv(f, a):
        total = None
        for b in range(3):
            term = dot(clip_im2col(tops, taps, f, b), weight[a, b].reshape(384, 256))
            total = term if total is None else total + term
        return total

    part[...] = (conv(2, 0) + conv(3, 1)).astype(part.dtype).reshape(4, 64, 256)
    lat1[...] = (conv(0, 0) + conv(1, 1) + conv(2, 2)).astype(BF16).reshape(4, 64, 256)
    own0[...] = conv(0, 2).reshape(4, 64, 256)
    tail[:, 0] = above[2:4]
    tail[:, 1:9] = clip[2:4]


def join_body(own0, part, lat1, cot, later_cot, lat, down, up):
    lat[0] = (own0[...] + part[...].astype(F32)).astype(BF16)
    lat[1] = lat1[...]
    down[:, 0:2] = lat[:, 2:4]
    down[:, 2, :, 0:128] = cot[:, 3]
    down[:, 2, :, 128:256] = later_cot[:, 3]
    up[:, 0:2] = lat[:, 0:2]
    up[:, 2, :, 0:128] = cot[:, 0]
    up[:, 2, :, 128:256] = later_cot[:, 0]


def fill_latent(lat, top, bottom, wide):
    for f in range(2):
        for r in range(2):
            wide[f, r] = jnp.concatenate(neighbour_cols(top[f, r]), axis=1)
            wide[f, 6 + r] = jnp.concatenate(neighbour_cols(bottom[f, r]), axis=1)

        def one(r, carry, f=f):
            wide[f, r + 2] = jnp.concatenate(neighbour_cols(lat[f, r]), axis=1)
            return carry

        lax.fori_loop(0, 4, one, 0)


def decode_body(lat, top, bottom, weight, own, behind, part, wide):
    fill_latent(lat, top, bottom, wide)

    def conv(f, a):
        total = None
        for b in range(3):
            window = wide[f, b : b + 6].reshape(384, 768)
            term = dot(window, weight[a, b].reshape(768, 128))
            total = term if total is None else total + term
        return total

    part[0] = (conv(0, 0) + conv(1, 1)).astype(part.dtype).reshape(6, 64, 128)
    part[1] = conv(1, 0).astype(part.dtype).reshape(6, 64, 128)
    own[0] = conv(0, 2).reshape(6, 64, 128)
    own[1] = (conv(0, 1) + conv(1, 2)).reshape(6, 64, 128)
    behind[...] = own[...].astype(behind.dtype)


def turned_body(seg_at, tail, tops, taps, lat, top, bottom, turned, btops, btaps, wide, stage):
    seg = seg_at[0]

    @pl.when(seg == 0)
    def _():
        start_stage(stage)
        for f in range(2):
            btops[f] = clip_windows(tail[f, 0], stage)

            def one(r, carry, f=f):
                btaps[f, r] = clip_windows(tail[f, r + 1], stage)
                return carry

            lax.fori_loop(0, 8, one, 0)
        for f in range(5):
            for b in range(3):
                rows = clip_im2col(btops, btaps, f, b) if f < 2 else clip_im2col(tops, taps, f - 2, b)
                turned[f * 3 + b] = rows.T

    @pl.when(seg != 0)
    def _():
        fill_latent(lat, top, bottom, wide)
        for f in range(2):
            for b in range(3):
                flat = wide[f, b + 1 : b + 5].reshape(256, 768).T
                turned[(f * 3 + b) * 2] = flat[0:384]
                turned[(f * 3 + b) * 2 + 1] = flat[384:768]


def grads_body(
    seg_at, core_at, own_part, from_behind, gone, from_later, cot, later_cot, top, bottom,
    weight, turned,
    lat_grad, own, send, gathered, slopes, rim,
):
    seg = seg_at[0]
    core = core_at[0]

    def slope_at(start, rows, pre, grad):
        sigm = jax.nn.sigmoid(pre[:, rows])
        scaled = grad.astype(F32) * sigm * (1.0 + pre[:, rows] * (1.0 - sigm))
        slopes[start : start + 2, rows] = scaled.astype(BF16)

    for start, one, other, mid, lanes in (
        (0, own_part, from_behind, cot, slice(0, 128)),
        (2, from_later, gone, later_cot, slice(128, 256)),
    ):
        pre = one[...].astype(F32) + other[...].astype(F32)
        slope_at(start, slice(0, 1), pre, top[:, 2:3, :, lanes])
        slope_at(start, slice(1, 5), pre, mid[...])
        slope_at(start, slice(5, 6), pre, bottom[:, 2:3, :, lanes])

    @pl.when(seg == 0)
    def _():
        for f in range(4):
            for r in range(6):
                left, same, right = neighbour_cols(slopes[f, r])
                rim[f, r] = jnp.concatenate([right, same, left], axis=1)
        grads = []
        for t in range(2):
            total = None
            for a in range(3):
                for b in range(3):
                    window = rim[t + 2 - a, 2 - b : 6 - b].reshape(256, 384)
                    side = jnp.concatenate([weight[a, b, c] for c in range(3)], axis=1)
                    term = dot_nt(window, side)
                    total = term if total is None else total + term
            grad = total.astype(BF16)
            lat_grad[t] = grad.reshape(4, 64, 256)
            grads.append(grad)
        for a in range(3):
            for b in range(3):
                total = dot(turned[a * 3 + b], grads[0]) + dot(turned[(a + 2) * 3 + b], grads[1])
                for c in range(3):
                    tap = (a * 3 + b) * 3 + c
                    for j in range(2):
                        gathered[pl.ds(tap * 256 + j, 128, stride=2), :] = total[
                            c * 128 : (c + 1) * 128, j * 128 : (j + 1) * 128
                        ]

    @pl.when(seg != 0)
    def _():
        lat_grad[...] = jnp.zeros(lat_grad.shape, BF16)
        for a in range(3):
            for b in range(3):
                for i in range(2):
                    total = None
                    for f in range(2):
                        cells = slopes[f + 2 - a, 1:5].reshape(256, 128)
                        term = dot(turned[(f * 3 + b) * 2 + i], cells)
                        total = term if total is None else total + term
                    start = (a * 3 + b) * 768 + i * 384
                    gathered[start : start + 384, :] = total

    half = own.shape[0]
    own[...] = gathered[pl.ds(pl.multiple_of(core * half, 8), half), :]
    send[...] = gathered[pl.ds(pl.multiple_of((1 - core) * half, 8), half), :].astype(BF16)


def halves_body(own, got, spread):
    for j in range(16):
        rows = slice(216 * j, 216 * (j + 1))
        spread[j] = (own[rows, :] + got[rows, :].astype(F32)).astype(BF16)


def second_body(got, spread):
    total = got[0].astype(F32)
    for j in range(1, 16):
        total = total + got[j].astype(F32)
    for j in range(4):
        spread[j] = total.astype(BF16)


def third_body(got, spread):
    total = got[0].astype(F32)
    for j in range(1, 4):
        total = total + got[j].astype(F32)
    for j in range(16):
        spread[j] = total.astype(BF16)


def exchanged(array, axes):
    return lax.all_to_all(array, axes, 0, 0, tiled=True)


def to_core(array):
    return lax.ppermute(array, "c", [(0, 1), (1, 0)])


def by_frames(array, by):
    pairs = [(i, i + by) for i in range(16) if 0 <= i + by < 16]
    return lax.ppermute(array, ("x", "z"), pairs)


def by_rows(array, by):
    pairs = [(i, i + by) for i in range(8) if 0 <= i + by < 8]
    return lax.ppermute(array, ("y", "c"), pairs)


def pair_body(seg_at, lat_grad, latent, pair):
    pair[...] = jnp.where(seg_at[0] == 0, lat_grad[...], latent[...])


def scaled_body(core_at, half, out):
    out[0] = half[...].astype(F32) * (1.0 / math.sqrt(32 * 32 * 64))


def half_written(core_at, half):
    return pl.pallas_call(
        scaled_body,
        out_shape=shape((2, 3456, 128), F32),
        grid_spec=pltpu.PrefetchScalarGridSpec(
            num_scalar_prefetch=1,
            grid=(4,),
            in_specs=[pl.BlockSpec((864, 128), lambda i, core: (i, 0))],
            out_specs=pl.BlockSpec((1, 864, 128), lambda i, core: (core[0], i, 0)),
        ),
        name="half_written",
        compiler_params=pltpu.CompilerParams(vmem_limit_bytes=8 * MIB),
    )(core_at, half)


def other_body(core_at, half, written, out):
    scaled_body(core_at, half, out)


def other_written(core_at, half, written):
    return pl.pallas_call(
        other_body,
        out_shape=shape((2, 3456, 128), F32),
        grid_spec=pltpu.PrefetchScalarGridSpec(
            num_scalar_prefetch=1,
            grid=(4,),
            in_specs=[
                pl.BlockSpec((864, 128), lambda i, core: (i, 0)),
                pl.BlockSpec(memory_space=pl.ANY),
            ],
            out_specs=pl.BlockSpec((1, 864, 128), lambda i, core: (1 - core[0], i, 0)),
        ),
        input_output_aliases={2: 0},
        name="other_written",
        compiler_params=pltpu.CompilerParams(vmem_limit_bytes=8 * MIB),
    )(core_at, half, written)


def summed(own, send):
    got = to_core(send)
    (wide,) = on_chip(halves_body, [shape((16, 216, 128), BF16)])(own, got)
    (thin,) = on_chip(second_body, [shape((4, 216, 128), BF16)])(exchanged(wide, ("x", "y")))
    (wide,) = on_chip(third_body, [shape((16, 216, 128), BF16)])(exchanged(thin, "z"))
    half = exchanged(wide, ("x", "y")).reshape(3456, 128)
    other = to_core(half)
    return half, other


def on_device(clip_frames, enc_weight, dec_weight, out_grad):
    seg = lax.axis_index("segment")
    core = lax.axis_index("c")

    stage = pltpu.VMEM((136, 128), F32)
    seg = seg.reshape(1)
    core_at = core.reshape(1)
    (down,) = on_chip(edge_body, [shape((4, 128, 128), BF16)], 2)(seg, core_at, clip_frames)
    above = by_rows(down, 1)
    (taps,) = on_chip(windows_body, [shape((4, 8, 64, 384), BF16)], scratch=[stage])(clip_frames)
    lat1, part, own0, tops, tail = on_chip(
        encode_body,
        [
            shape((4, 64, 256), BF16),
            shape((4, 64, 256), PART),
            shape((4, 64, 256), F32),
            shape((4, 64, 384), BF16),
            shape((2, 9, 128, 128), BF16),
        ],
        scratch=[stage],
        grant=16,
    )(clip_frames, taps, above, enc_weight)
    part = by_frames(part, 1)
    later_cot = by_frames(out_grad, -1)
    latent, down, up = on_chip(
        join_body,
        [
            shape((2, 4, 64, 256), BF16),
            shape((2, 3, 64, 256), BF16),
            shape((2, 3, 64, 256), BF16),
        ],
    )(own0, part, lat1, out_grad, later_cot)
    top = by_rows(down, 1)
    bottom = by_rows(up, -1)
    pairs = [(16 + t - 1, t) for t in range(1, 16)]
    tail = lax.ppermute(tail, ("segment", "x", "z"), pairs)
    rows6 = (2, 6, 64, 128)
    own_part, behind, gone = on_chip(
        decode_body,
        [shape(rows6, F32), shape(rows6, PART), shape(rows6, PART)],
        scratch=[pltpu.VMEM((2, 8, 64, 768), BF16)],
        grant=14,
    )(latent, top, bottom, dec_weight)
    from_behind = by_frames(gone, 1)
    from_later = by_frames(behind, -1)
    tail, lat, _ = lax.optimization_barrier((tail, latent, gone))
    (turned,) = on_chip(
        turned_body,
        [shape((15, 384, 256), BF16)],
        1,
        [
            pltpu.VMEM((2, 64, 384), BF16),
            pltpu.VMEM((2, 8, 64, 384), BF16),
            pltpu.VMEM((2, 8, 64, 768), BF16),
            stage,
        ],
        16,
    )(seg, tail, tops, taps, lat, top, bottom)
    lat_grad, own, send = on_chip(
        grads_body,
        [
            shape((2, 4, 64, 256), BF16),
            shape((3456, 128), F32),
            shape((3456, 128), BF16),
        ],
        2,
        [
            pltpu.VMEM((6912, 128), F32),
            pltpu.VMEM((4, 6, 64, 128), BF16),
            pltpu.VMEM((4, 6, 64, 384), BF16),
        ],
        24,
    )(seg, core_at, own_part, from_behind, gone, from_later, out_grad, later_cot, top, bottom, dec_weight, turned)
    (latent_pair,) = on_chip(pair_body, [shape((2, 4, 64, 256), BF16)], 1)(seg, lat_grad, latent)
    half, other = summed(own, send)
    grads = half_written(core_at, half)
    grads = other_written(core_at, other, grads)
    return latent_pair[None], grads.reshape(1, 27, 32768)


def solution(mesh):
    fine = Mesh(mesh.devices.reshape(2, 4, 4, 4, 2), ("segment", "x", "z", "y", "c"))
    cells = P(("x", "z"), ("y", "c"), None, None)

    return jax.shard_map(
        on_device,
        mesh=fine,
        in_specs=(cells, P(), P(), cells),
        out_specs=(P("segment", ("x", "z"), ("y", "c"), None, None), P("segment", None, None)),
        check_vma=False,
    )
```

```python
import math

import jax
import jax.numpy as jnp
from jax import lax
from jax.experimental import pallas as pl
from jax.experimental.pallas import tpu as pltpu
from jax.sharding import Mesh, PartitionSpec as P

F32 = jnp.float32
BF16 = jnp.bfloat16
PART = BF16
MIB = 1024 * 1024


def shape(dims, dtype):
    return jax.ShapeDtypeStruct(dims, dtype)


def on_chip(body, outs, smem=0, scratch=(), grant=8):
    def call(*args):
        specs = [pl.BlockSpec(memory_space=pltpu.SMEM)] * smem
        specs += [pl.BlockSpec(memory_space=pltpu.VMEM)] * (len(args) - smem)
        return pl.pallas_call(
            body,
            out_shape=outs,
            in_specs=specs,
            out_specs=[pl.BlockSpec(memory_space=pltpu.VMEM)] * len(outs),
            scratch_shapes=list(scratch),
            compiler_params=pltpu.CompilerParams(vmem_limit_bytes=grant * MIB),
        )(*args)

    return call


def dot(left, right):
    return jnp.dot(left, right, preferred_element_type=F32)


def dot_nt(left, right):
    return lax.dot_general(left, right, (((1,), (1,)), ((), ())), preferred_element_type=F32)


def clip_windows(row, stage):
    stage[8:136, :] = row.astype(F32)
    before = stage[pl.ds(7, 64, stride=2), :]
    here = stage[pl.ds(8, 64, stride=2), :]
    after = stage[pl.ds(9, 64, stride=2), :]
    return jnp.concatenate([before, here, after], axis=1).astype(BF16)


def neighbour_cols(row):
    wide = row.astype(F32)
    place = lax.broadcasted_iota(jnp.int32, wide.shape, 0)
    last = wide.shape[0] - 1
    before = jnp.where(place == 0, 0.0, pltpu.roll(wide, 1, 0)).astype(BF16)
    after = jnp.where(place == last, 0.0, pltpu.roll(wide, last, 0)).astype(BF16)
    return before, row, after


def start_stage(stage):
    stage[0:8, :] = jnp.zeros((8, stage.shape[1]), F32)


def edge_body(seg_at, core_at, clip, down):
    down[...] = clip[:, 7]


def windows_body(clip, taps, stage):
    start_stage(stage)
    for f in range(4):

        def one(r, carry, f=f):
            taps[f, r] = clip_windows(clip[f, r], stage)
            return carry

        lax.fori_loop(0, 8, one, 0)


def clip_im2col(tops, taps, f, b):
    rows = [2 * h + b for h in range(4)]
    return jnp.concatenate([tops[f] if p == 0 else taps[f, p - 1] for p in rows], axis=0)


def encode_body(
    clip, taps, above, weight, lat1, part, own0, tops, tail, stage
):
    start_stage(stage)
    for f in range(4):
        tops[f] = clip_windows(above[f], stage)

    def conv(frames, a):
        total = None
        for b in range(3):
            rows = jnp.concatenate([clip_im2col(tops, taps, f, b) for f in frames], axis=0)
            term = dot(rows, weight[a, b].reshape(384, 256))
            total = term if total is None else total + term
        return total[0:256], total[256:512]

    (one, two), (three, four), (five, six) = conv((0, 2), 0), conv((1, 3), 1), conv((0, 2), 2)
    part[...] = (two + four).astype(part.dtype).reshape(4, 64, 256)
    lat1[...] = (one + three + six).astype(BF16).reshape(4, 64, 256)
    own0[...] = five.reshape(4, 64, 256)
    tail[:, 0] = above[2:4]
    tail[:, 1:9] = clip[2:4]


def join_body(own0, part, lat1, cot, later_cot, lat, down, up):
    lat[0] = (own0[...] + part[...].astype(F32)).astype(BF16)
    lat[1] = lat1[...]
    down[:, 0:2] = lat[:, 2:4]
    down[:, 2, :, 0:128] = cot[:, 3]
    down[:, 2, :, 128:256] = later_cot[:, 3]
    up[:, 0:2] = lat[:, 0:2]
    up[:, 2, :, 0:128] = cot[:, 0]
    up[:, 2, :, 128:256] = later_cot[:, 0]


def fill_latent(lat, top, bottom, wide):
    for f in range(2):
        for r in range(2):
            wide[f, r] = jnp.concatenate(neighbour_cols(top[f, r]), axis=1)
            wide[f, 6 + r] = jnp.concatenate(neighbour_cols(bottom[f, r]), axis=1)

        def one(r, carry, f=f):
            wide[f, r + 2] = jnp.concatenate(neighbour_cols(lat[f, r]), axis=1)
            return carry

        lax.fori_loop(0, 4, one, 0)


def decode_body(lat, top, bottom, weight, own, behind, part, wide):
    fill_latent(lat, top, bottom, wide)

    def conv(a):
        total = None
        for b in range(3):
            window = wide[:, b : b + 6].reshape(768, 768)
            term = dot(window, weight[a, b].reshape(768, 128))
            total = term if total is None else total + term
        return total.reshape(2, 6, 64, 128)

    one, two, three = conv(0), conv(1), conv(2)
    part[0] = (one[0] + two[1]).astype(part.dtype)
    part[1] = one[1].astype(part.dtype)
    own[0] = three[0]
    own[1] = two[0] + three[1]
    behind[...] = own[...].astype(behind.dtype)


def turned_body(seg_at, tail, tops, taps, lat, top, bottom, turned, btops, btaps, wide, stage):
    seg = seg_at[0]

    @pl.when(seg == 0)
    def _():
        start_stage(stage)
        for f in range(2):
            btops[f] = clip_windows(tail[f, 0], stage)

            def one(r, carry, f=f):
                btaps[f, r] = clip_windows(tail[f, r + 1], stage)
                return carry

            lax.fori_loop(0, 8, one, 0)
        for f in range(5):
            for b in range(3):
                rows = clip_im2col(btops, btaps, f, b) if f < 2 else clip_im2col(tops, taps, f - 2, b)
                turned[f * 3 + b] = rows.T

    @pl.when(seg != 0)
    def _():
        fill_latent(lat, top, bottom, wide)
        for f in range(2):
            for b in range(3):
                flat = wide[f, b + 1 : b + 5].reshape(256, 768).T
                turned[(f * 3 + b) * 2] = flat[0:384]
                turned[(f * 3 + b) * 2 + 1] = flat[384:768]


def grads_body(
    seg_at, core_at, own_part, from_behind, gone, from_later, cot, later_cot, top, bottom,
    weight, turned,
    lat_grad, own, send, gathered, slopes, rim,
):
    seg = seg_at[0]
    core = core_at[0]

    def slope_at(start, rows, pre, grad):
        sigm = jax.nn.sigmoid(pre[:, rows])
        scaled = grad.astype(F32) * sigm * (1.0 + pre[:, rows] * (1.0 - sigm))
        slopes[start : start + 2, rows] = scaled.astype(BF16)

    for start, one, other, mid, lanes in (
        (0, own_part, from_behind, cot, slice(0, 128)),
        (2, from_later, gone, later_cot, slice(128, 256)),
    ):
        pre = one[...].astype(F32) + other[...].astype(F32)
        slope_at(start, slice(0, 1), pre, top[:, 2:3, :, lanes])
        slope_at(start, slice(1, 5), pre, mid[...])
        slope_at(start, slice(5, 6), pre, bottom[:, 2:3, :, lanes])

    @pl.when(seg == 0)
    def _():
        for f in range(4):
            for r in range(6):
                left, same, right = neighbour_cols(slopes[f, r])
                rim[f, r] = jnp.concatenate([right, same, left], axis=1)
        total = None
        for a in range(3):
            for b in range(3):
                window = rim[2 - a : 4 - a, 2 - b : 6 - b].reshape(512, 384)
                side = jnp.concatenate([weight[a, b, c] for c in range(3)], axis=1)
                term = dot_nt(window, side)
                total = term if total is None else total + term
        grad = total.astype(BF16)
        lat_grad[...] = grad.reshape(2, 4, 64, 256)
        grads = (grad[0:256], grad[256:512])
        for a in range(3):
            for b in range(3):
                total = dot(turned[a * 3 + b], grads[0]) + dot(turned[(a + 2) * 3 + b], grads[1])
                for c in range(3):
                    tap = (a * 3 + b) * 3 + c
                    for j in range(2):
                        gathered[pl.ds(tap * 256 + j, 128, stride=2), :] = total[
                            c * 128 : (c + 1) * 128, j * 128 : (j + 1) * 128
                        ]

    @pl.when(seg != 0)
    def _():
        lat_grad[...] = jnp.zeros(lat_grad.shape, BF16)
        for a in range(3):
            for b in range(3):
                for i in range(2):
                    total = None
                    for f in range(2):
                        cells = slopes[f + 2 - a, 1:5].reshape(256, 128)
                        term = dot(turned[(f * 3 + b) * 2 + i], cells)
                        total = term if total is None else total + term
                    start = (a * 3 + b) * 768 + i * 384
                    gathered[start : start + 384, :] = total

    half = own.shape[0]
    own[...] = gathered[pl.ds(pl.multiple_of(core * half, 8), half), :]
    send[...] = gathered[pl.ds(pl.multiple_of((1 - core) * half, 8), half), :].astype(BF16)


def halves_body(own, got, spread):
    for j in range(16):
        rows = slice(216 * j, 216 * (j + 1))
        spread[j] = (own[rows, :] + got[rows, :].astype(F32)).astype(BF16)


def second_body(got, spread):
    total = got[0].astype(F32)
    for j in range(1, 16):
        total = total + got[j].astype(F32)
    for j in range(4):
        spread[j] = total.astype(BF16)


def third_body(got, spread):
    total = got[0].astype(F32)
    for j in range(1, 4):
        total = total + got[j].astype(F32)
    for j in range(16):
        spread[j] = total.astype(BF16)


def exchanged(array, axes):
    return lax.all_to_all(array, axes, 0, 0, tiled=True)


def to_core(array):
    return lax.ppermute(array, "c", [(0, 1), (1, 0)])


def by_frames(array, by):
    pairs = [(i, i + by) for i in range(16) if 0 <= i + by < 16]
    return lax.ppermute(array, ("x", "z"), pairs)


def by_rows(array, by):
    pairs = [(i, i + by) for i in range(8) if 0 <= i + by < 8]
    return lax.ppermute(array, ("y", "c"), pairs)


def pair_body(seg_at, lat_grad, latent, pair):
    pair[...] = jnp.where(seg_at[0] == 0, lat_grad[...], latent[...])


def write_half(at, half, out, held, sent):
    copies = []
    for i in range(4):
        rows = pl.ds(864 * i, 864)
        held[rows, :] = half[rows, :].astype(F32) * (1.0 / math.sqrt(32 * 32 * 64))
        copies.append(pltpu.make_async_copy(held.at[rows], out.at[at, rows], sent.at[i]))
        copies[-1].start()
    for one in copies:
        one.wait()


def half_body(core_at, half, out, held, sent):
    write_half(core_at[0], half, out, held, sent)


def other_body(core_at, half, written, out, held, sent):
    write_half(1 - core_at[0], half, out, held, sent)


def written(body, core_at, half, *given):
    specs = [pl.BlockSpec(memory_space=pltpu.SMEM), pl.BlockSpec(memory_space=pltpu.VMEM)]
    return pl.pallas_call(
        body,
        out_shape=shape((2, 3456, 128), F32),
        in_specs=specs + [pl.BlockSpec(memory_space=pl.ANY)] * len(given),
        out_specs=pl.BlockSpec(memory_space=pl.ANY),
        scratch_shapes=[pltpu.VMEM((3456, 128), F32), pltpu.SemaphoreType.DMA((4,))],
        input_output_aliases={2: 0} if given else {},
        compiler_params=pltpu.CompilerParams(vmem_limit_bytes=8 * MIB),
    )(core_at, half, *given)


def summed(own, send):
    got = to_core(send)
    (wide,) = on_chip(halves_body, [shape((16, 216, 128), BF16)])(own, got)
    (thin,) = on_chip(second_body, [shape((4, 216, 128), BF16)])(exchanged(wide, ("x", "y")))
    (wide,) = on_chip(third_body, [shape((16, 216, 128), BF16)])(exchanged(thin, "z"))
    half = exchanged(wide, ("x", "y")).reshape(3456, 128)
    other = to_core(half)
    return half, other


def on_device(clip_frames, enc_weight, dec_weight, out_grad):
    seg = lax.axis_index("segment")
    core = lax.axis_index("c")

    stage = pltpu.VMEM((136, 128), F32)
    seg = seg.reshape(1)
    core_at = core.reshape(1)
    (down,) = on_chip(edge_body, [shape((4, 128, 128), BF16)], 2)(seg, core_at, clip_frames)
    above = by_rows(down, 1)
    (taps,) = on_chip(windows_body, [shape((4, 8, 64, 384), BF16)], scratch=[stage])(clip_frames)
    lat1, part, own0, tops, tail = on_chip(
        encode_body,
        [
            shape((4, 64, 256), BF16),
            shape((4, 64, 256), PART),
            shape((4, 64, 256), F32),
            shape((4, 64, 384), BF16),
            shape((2, 9, 128, 128), BF16),
        ],
        scratch=[stage],
        grant=16,
    )(clip_frames, taps, above, enc_weight)
    part = by_frames(part, 1)
    later_cot = by_frames(out_grad, -1)
    latent, down, up = on_chip(
        join_body,
        [
            shape((2, 4, 64, 256), BF16),
            shape((2, 3, 64, 256), BF16),
            shape((2, 3, 64, 256), BF16),
        ],
    )(own0, part, lat1, out_grad, later_cot)
    top = by_rows(down, 1)
    bottom = by_rows(up, -1)
    pairs = [(16 + t - 1, t) for t in range(1, 16)]
    tail = lax.ppermute(tail, ("segment", "x", "z"), pairs)
    rows6 = (2, 6, 64, 128)
    own_part, behind, gone = on_chip(
        decode_body,
        [shape(rows6, F32), shape(rows6, PART), shape(rows6, PART)],
        scratch=[pltpu.VMEM((2, 8, 64, 768), BF16)],
        grant=14,
    )(latent, top, bottom, dec_weight)
    from_behind = by_frames(gone, 1)
    from_later = by_frames(behind, -1)
    tail, lat, _ = lax.optimization_barrier((tail, latent, gone))
    (turned,) = on_chip(
        turned_body,
        [shape((15, 384, 256), BF16)],
        1,
        [
            pltpu.VMEM((2, 64, 384), BF16),
            pltpu.VMEM((2, 8, 64, 384), BF16),
            pltpu.VMEM((2, 8, 64, 768), BF16),
            stage,
        ],
        16,
    )(seg, tail, tops, taps, lat, top, bottom)
    lat_grad, own, send = on_chip(
        grads_body,
        [
            shape((2, 4, 64, 256), BF16),
            shape((3456, 128), F32),
            shape((3456, 128), BF16),
        ],
        2,
        [
            pltpu.VMEM((6912, 128), F32),
            pltpu.VMEM((4, 6, 64, 128), BF16),
            pltpu.VMEM((4, 6, 64, 384), BF16),
        ],
        24,
    )(seg, core_at, own_part, from_behind, gone, from_later, out_grad, later_cot, top, bottom, dec_weight, turned)
    (latent_pair,) = on_chip(pair_body, [shape((2, 4, 64, 256), BF16)], 1)(seg, lat_grad, latent)
    half, other = summed(own, send)
    grads = written(half_body, core_at, half)
    grads = written(other_body, core_at, other, grads)
    return latent_pair[None], grads.reshape(1, 27, 32768)


def solution(mesh):
    fine = Mesh(mesh.devices.reshape(2, 4, 4, 4, 2), ("segment", "x", "z", "y", "c"))
    cells = P(("x", "z"), ("y", "c"), None, None)

    return jax.shard_map(
        on_device,
        mesh=fine,
        in_specs=(cells, P(), P(), cells),
        out_specs=(P("segment", ("x", "z"), ("y", "c"), None, None), P("segment", None, None)),
        check_vma=False,
    )
```

```python
import math

import jax
import jax.numpy as jnp
from jax import lax
from jax.experimental import pallas as pl
from jax.experimental.pallas import tpu as pltpu
from jax.sharding import Mesh, PartitionSpec as P

F32 = jnp.float32
BF16 = jnp.bfloat16
PART = BF16
MIB = 1024 * 1024


def shape(dims, dtype):
    return jax.ShapeDtypeStruct(dims, dtype)


def on_chip(body, outs, smem=0, scratch=(), grant=8):
    def call(*args):
        specs = [pl.BlockSpec(memory_space=pltpu.SMEM)] * smem
        specs += [pl.BlockSpec(memory_space=pltpu.VMEM)] * (len(args) - smem)
        return pl.pallas_call(
            body,
            out_shape=outs,
            in_specs=specs,
            out_specs=[pl.BlockSpec(memory_space=pltpu.VMEM)] * len(outs),
            scratch_shapes=list(scratch),
            compiler_params=pltpu.CompilerParams(vmem_limit_bytes=grant * MIB),
        )(*args)

    return call


def dot(left, right):
    return jnp.dot(left, right, preferred_element_type=F32)


def dot_nt(left, right):
    return lax.dot_general(left, right, (((1,), (1,)), ((), ())), preferred_element_type=F32)


def clip_windows(row, stage):
    stage[8:136, :] = row.astype(F32)
    before = stage[pl.ds(7, 64, stride=2), :]
    here = stage[pl.ds(8, 64, stride=2), :]
    after = stage[pl.ds(9, 64, stride=2), :]
    return jnp.concatenate([before, here, after], axis=1).astype(BF16)


def neighbour_cols(row):
    wide = row.astype(F32)
    place = lax.broadcasted_iota(jnp.int32, wide.shape, 0)
    last = wide.shape[0] - 1
    before = jnp.where(place == 0, 0.0, pltpu.roll(wide, 1, 0)).astype(BF16)
    after = jnp.where(place == last, 0.0, pltpu.roll(wide, last, 0)).astype(BF16)
    return before, row, after


def start_stage(stage):
    stage[0:8, :] = jnp.zeros((8, stage.shape[1]), F32)


def edge_body(seg_at, core_at, clip, cot, down, up):
    down[0:4] = clip[:, 7]
    down[4, 0:64] = cot[0, 3]
    down[4, 64:128] = cot[1, 3]
    up[...] = cot[:, 0]


def windows_body(clip, taps, stage):
    start_stage(stage)
    for f in range(4):

        def one(r, carry, f=f):
            taps[f, r] = clip_windows(clip[f, r], stage)
            return carry

        lax.fori_loop(0, 8, one, 0)


def clip_im2col(tops, taps, f, b):
    rows = [2 * h + b for h in range(4)]
    return jnp.concatenate([tops[f] if p == 0 else taps[f, p - 1] for p in rows], axis=0)


def encode_body(
    clip, taps, above, weight, cot, below, lat1, part, own0, tops, tail, rows6, stage
):
    start_stage(stage)
    for f in range(4):
        tops[f] = clip_windows(above[f], stage)

    def conv(f, a):
        total = None
        for b in range(3):
            term = dot(clip_im2col(tops, taps, f, b), weight[a, b].reshape(384, 256))
            total = term if total is None else total + term
        return total

    part[...] = (conv(2, 0) + conv(3, 1)).astype(part.dtype).reshape(4, 64, 256)
    lat1[...] = (conv(0, 0) + conv(1, 1) + conv(2, 2)).astype(BF16).reshape(4, 64, 256)
    own0[...] = conv(0, 2).reshape(4, 64, 256)
    tail[:, 0] = above[2:4]
    tail[:, 1:9] = clip[2:4]
    rows6[0, 0] = above[4, 0:64]
    rows6[1, 0] = above[4, 64:128]
    rows6[:, 1:5] = cot[...]
    rows6[:, 5] = below[...]


def join_body(own0, part, lat1, lat, down, up):
    lat[0] = (own0[...] + part[...].astype(F32)).astype(BF16)
    lat[1] = lat1[...]
    down[...] = lat[:, 2:4]
    up[...] = lat[:, 0:2]


def fill_latent(lat, top, bottom, wide):
    for f in range(2):
        for r in range(2):
            wide[f, r] = jnp.concatenate(neighbour_cols(top[f, r]), axis=1)
            wide[f, 6 + r] = jnp.concatenate(neighbour_cols(bottom[f, r]), axis=1)

        def one(r, carry, f=f):
            wide[f, r + 2] = jnp.concatenate(neighbour_cols(lat[f, r]), axis=1)
            return carry

        lax.fori_loop(0, 4, one, 0)


def decode_body(lat, top, bottom, weight, own, behind, part, wide):
    fill_latent(lat, top, bottom, wide)

    def conv(f, a):
        total = None
        for b in range(3):
            window = wide[f, b : b + 6].reshape(384, 768)
            term = dot(window, weight[a, b].reshape(768, 128))
            total = term if total is None else total + term
        return total

    part[0] = (conv(0, 0) + conv(1, 1)).astype(part.dtype).reshape(6, 64, 128)
    part[1] = conv(1, 0).astype(part.dtype).reshape(6, 64, 128)
    own[0] = conv(0, 2).reshape(6, 64, 128)
    own[1] = (conv(0, 1) + conv(1, 2)).reshape(6, 64, 128)
    behind[...] = own[...].astype(behind.dtype)


def turned_body(seg_at, tail, tops, taps, lat, top, bottom, turned, btops, btaps, wide, stage):
    seg = seg_at[0]

    @pl.when(seg == 0)
    def _():
        start_stage(stage)
        for f in range(2):
            btops[f] = clip_windows(tail[f, 0], stage)

            def one(r, carry, f=f):
                btaps[f, r] = clip_windows(tail[f, r + 1], stage)
                return carry

            lax.fori_loop(0, 8, one, 0)
        for f in range(5):
            for b in range(3):
                rows = clip_im2col(btops, btaps, f, b) if f < 2 else clip_im2col(tops, taps, f - 2, b)
                turned[f * 3 + b] = rows.T

    @pl.when(seg != 0)
    def _():
        fill_latent(lat, top, bottom, wide)
        for f in range(2):
            for b in range(3):
                flat = wide[f, b + 1 : b + 5].reshape(256, 768).T
                turned[(f * 3 + b) * 2] = flat[0:384]
                turned[(f * 3 + b) * 2 + 1] = flat[384:768]


def grads_body(
    seg_at, core_at, own_part, from_behind, gone, from_later, cot, later_cot, weight, turned,
    lat_grad, own, send, gathered, slopes, rim,
):
    seg = seg_at[0]
    core = core_at[0]

    def slope_of(pre, grad):
        sigm = jax.nn.sigmoid(pre)
        return (grad.astype(F32) * sigm * (1.0 + pre * (1.0 - sigm))).astype(BF16)

    slopes[0:2] = slope_of(own_part[...] + from_behind[...].astype(F32), cot[...])
    slopes[2:4] = slope_of(from_later[...].astype(F32) + gone[...].astype(F32), later_cot[...])

    @pl.when(seg == 0)
    def _():
        for f in range(4):
            for r in range(6):
                left, same, right = neighbour_cols(slopes[f, r])
                rim[f, r] = jnp.concatenate([right, same, left], axis=1)
        grads = []
        for t in range(2):
            total = None
            for a in range(3):
                for b in range(3):
                    window = rim[t + 2 - a, 2 - b : 6 - b].reshape(256, 384)
                    side = jnp.concatenate([weight[a, b, c] for c in range(3)], axis=1)
                    term = dot_nt(window, side)
                    total = term if total is None else total + term
            grad = total.astype(BF16)
            lat_grad[t] = grad.reshape(4, 64, 256)
            grads.append(grad)
        for a in range(3):
            for b in range(3):
                total = dot(turned[a * 3 + b], grads[0]) + dot(turned[(a + 2) * 3 + b], grads[1])
                for c in range(3):
                    tap = (a * 3 + b) * 3 + c
                    for j in range(2):
                        gathered[pl.ds(tap * 256 + j, 128, stride=2), :] = total[
                            c * 128 : (c + 1) * 128, j * 128 : (j + 1) * 128
                        ]

    @pl.when(seg != 0)
    def _():
        lat_grad[...] = jnp.zeros(lat_grad.shape, BF16)
        for a in range(3):
            for b in range(3):
                for i in range(2):
                    total = None
                    for f in range(2):
                        cells = slopes[f + 2 - a, 1:5].reshape(256, 128)
                        term = dot(turned[(f * 3 + b) * 2 + i], cells)
                        total = term if total is None else total + term
                    start = (a * 3 + b) * 768 + i * 384
                    gathered[start : start + 384, :] = total

    half = own.shape[0]
    own[...] = gathered[pl.ds(pl.multiple_of(core * half, 8), half), :]
    send[...] = gathered[pl.ds(pl.multiple_of((1 - core) * half, 8), half), :].astype(BF16)


def halves_body(own, got, spread):
    for j in range(16):
        rows = slice(216 * j, 216 * (j + 1))
        spread[j] = (own[rows, :] + got[rows, :].astype(F32)).astype(BF16)


def second_body(got, spread):
    total = got[0].astype(F32)
    for j in range(1, 16):
        total = total + got[j].astype(F32)
    for j in range(4):
        spread[j] = total.astype(BF16)


def third_body(got, spread):
    total = got[0].astype(F32)
    for j in range(1, 4):
        total = total + got[j].astype(F32)
    for j in range(16):
        spread[j] = total.astype(BF16)


def exchanged(array, axes):
    return lax.all_to_all(array, axes, 0, 0, tiled=True)


def to_core(array):
    return lax.ppermute(array, "c", [(0, 1), (1, 0)])


def by_frames(array, by):
    pairs = [(i, i + by) for i in range(16) if 0 <= i + by < 16]
    return lax.ppermute(array, ("x", "z"), pairs)


def by_rows(array, by):
    pairs = [(i, i + by) for i in range(8) if 0 <= i + by < 8]
    return lax.ppermute(array, ("y", "c"), pairs)


def pair_body(seg_at, lat_grad, latent, pair):
    pair[...] = jnp.where(seg_at[0] == 0, lat_grad[...], latent[...])


def write_half(at, half, out, held, sent):
    copies = []
    for i in range(4):
        rows = pl.ds(864 * i, 864)
        held[rows, :] = half[rows, :].astype(F32) * (1.0 / math.sqrt(32 * 32 * 64))
        copies.append(pltpu.make_async_copy(held.at[rows], out.at[at, rows], sent.at[i]))
        copies[-1].start()
    for one in copies:
        one.wait()


def half_body(core_at, half, out, held, sent):
    write_half(core_at[0], half, out, held, sent)


def other_body(core_at, half, written, out, held, sent):
    write_half(1 - core_at[0], half, out, held, sent)


def written(body, core_at, half, *given):
    specs = [pl.BlockSpec(memory_space=pltpu.SMEM), pl.BlockSpec(memory_space=pltpu.VMEM)]
    return pl.pallas_call(
        body,
        out_shape=shape((2, 3456, 128), F32),
        in_specs=specs + [pl.BlockSpec(memory_space=pl.ANY)] * len(given),
        out_specs=pl.BlockSpec(memory_space=pl.ANY),
        scratch_shapes=[pltpu.VMEM((3456, 128), F32), pltpu.SemaphoreType.DMA((4,))],
        input_output_aliases={2: 0} if given else {},
        compiler_params=pltpu.CompilerParams(vmem_limit_bytes=8 * MIB),
    )(core_at, half, *given)


def summed(own, send):
    got = to_core(send)
    (wide,) = on_chip(halves_body, [shape((16, 216, 128), BF16)])(own, got)
    (thin,) = on_chip(second_body, [shape((4, 216, 128), BF16)])(exchanged(wide, ("x", "y")))
    (wide,) = on_chip(third_body, [shape((16, 216, 128), BF16)])(exchanged(thin, "z"))
    half = exchanged(wide, ("x", "y")).reshape(3456, 128)
    other = to_core(half)
    return half, other


def on_device(clip_frames, enc_weight, dec_weight, out_grad):
    seg = lax.axis_index("segment")
    core = lax.axis_index("c")

    stage = pltpu.VMEM((136, 128), F32)
    seg = seg.reshape(1)
    core_at = core.reshape(1)
    down, up = on_chip(
        edge_body, [shape((5, 128, 128), BF16), shape((2, 64, 128), BF16)], 2
    )(seg, core_at, clip_frames, out_grad)
    above = by_rows(down, 1)
    below = by_rows(up, -1)
    (taps,) = on_chip(windows_body, [shape((4, 8, 64, 384), BF16)], scratch=[stage])(clip_frames)
    lat1, part, own0, tops, tail, cot = on_chip(
        encode_body,
        [
            shape((4, 64, 256), BF16),
            shape((4, 64, 256), PART),
            shape((4, 64, 256), F32),
            shape((4, 64, 384), BF16),
            shape((2, 9, 128, 128), BF16),
            shape((2, 6, 64, 128), BF16),
        ],
        scratch=[stage],
        grant=16,
    )(clip_frames, taps, above, enc_weight, out_grad, below)
    part = by_frames(part, 1)
    later_cot = by_frames(cot, -1)
    latent, down, up = on_chip(
        join_body,
        [
            shape((2, 4, 64, 256), BF16),
            shape((2, 2, 64, 256), BF16),
            shape((2, 2, 64, 256), BF16),
        ],
    )(own0, part, lat1)
    top = by_rows(down, 1)
    bottom = by_rows(up, -1)
    pairs = [(16 + t - 1, t) for t in range(1, 16)]
    tail = lax.ppermute(tail, ("segment", "x", "z"), pairs)
    rows6 = (2, 6, 64, 128)
    own_part, behind, gone = on_chip(
        decode_body,
        [shape(rows6, F32), shape(rows6, PART), shape(rows6, PART)],
        scratch=[pltpu.VMEM((2, 8, 64, 768), BF16)],
        grant=14,
    )(latent, top, bottom, dec_weight)
    from_behind = by_frames(gone, 1)
    from_later = by_frames(behind, -1)
    tail, lat, _ = lax.optimization_barrier((tail, latent, gone))
    (turned,) = on_chip(
        turned_body,
        [shape((15, 384, 256), BF16)],
        1,
        [
            pltpu.VMEM((2, 64, 384), BF16),
            pltpu.VMEM((2, 8, 64, 384), BF16),
            pltpu.VMEM((2, 8, 64, 768), BF16),
            stage,
        ],
        16,
    )(seg, tail, tops, taps, lat, top, bottom)
    lat_grad, own, send = on_chip(
        grads_body,
        [
            shape((2, 4, 64, 256), BF16),
            shape((3456, 128), F32),
            shape((3456, 128), BF16),
        ],
        2,
        [
            pltpu.VMEM((6912, 128), F32),
            pltpu.VMEM((4, 6, 64, 128), BF16),
            pltpu.VMEM((4, 6, 64, 384), BF16),
        ],
        24,
    )(seg, core_at, own_part, from_behind, gone, from_later, cot, later_cot, dec_weight, turned)
    (latent_pair,) = on_chip(pair_body, [shape((2, 4, 64, 256), BF16)], 1)(seg, lat_grad, latent)
    half, other = summed(own, send)
    grads = written(half_body, core_at, half)
    grads = written(other_body, core_at, other, grads)
    return latent_pair[None], grads.reshape(1, 27, 32768)


def solution(mesh):
    fine = Mesh(mesh.devices.reshape(2, 4, 4, 4, 2), ("segment", "x", "z", "y", "c"))
    cells = P(("x", "z"), ("y", "c"), None, None)

    return jax.shard_map(
        on_device,
        mesh=fine,
        in_specs=(cells, P(), P(), cells),
        out_specs=(P("segment", ("x", "z"), ("y", "c"), None, None), P("segment", None, None)),
        check_vma=False,
    )
```
